128 devices in a mesh: gx: 8 (over x_hi, y), gy: 4 (over z), gz: 4 (over x_lo, core).
Axes of the slice: x: 4 (x_hi: 2, x_lo: 2; x = x_hi * 2 + x_lo), y: 4, z: 4, core: 2. Of those that a mesh axis runs over, the one named last changes fastest.
Arguments:
- features: bfloat16 [64, 32, 128, 128], P('gx', 'gy', 'gz'), may hold values from -6 to 6
- cotangent: bfloat16 [64, 32, 128, 128], P('gx', 'gy', 'gz'), may hold values from -6 to 6
- voxel_mask: int32 [64, 32, 128], P('gx', 'gy', 'gz'), may hold values 0 or 1
- brick_active: int32 [8, 4, 16], P('gx', 'gy', 'gz'), may hold values 0 or 1
- first_weight: bfloat16 [27, 128, 128], replicated, may hold values from -0.109375 to 0.109375
- second_weight: bfloat16 [27, 128, 128], replicated, may hold values from -0.109375 to 0.109375
Outputs:
- output_field: bfloat16 [64, 32, 128, 128], P('gx', 'gy', 'gz')
- grad_features: bfloat16 [64, 32, 128, 128], P('gx', 'gy', 'gz')
- grad_first: float32 [27, 128, 128], P(None, 'gx', ('gy', 'gz'))
- grad_second: float32 [27, 128, 128], P(None, 'gx', ('gy', 'gz'))
The draws below stay inside these ranges and needn't reach their ends.
All inputs are finite; a program needn't handle non-finite values. No bound on the sum of `voxel_mask` or of `brick_active` on one device may be relied on, other than what follows from the above.
Results may differ from the reference program's by a relative error of at most 0.005.
Values may be sent and summed in bfloat16 or wider, within the bound.
No kernel may reach another device: no remote copies, remote signals or barrier semaphores. Data moves between devices by JAX's collectives and lax.ppermute only.
A program may use at most 256 MiB of HBM per device.

```python
import math
import jax
import jax.numpy as jnp
from jax import lax

C = 128
BRICK = 8
NX = 64
NY = 32
NZ = 128


def place_ends(entries, key, low, top_value):
    longest = entries.shape.index(max(entries.shape))
    spots = []
    for shift in (0, 1):
        where = [jax.random.randint(jax.random.fold_in(key, axis), (), 0, length) for axis, length in enumerate(entries.shape)]
        where[longest] = (where[longest] + shift) % entries.shape[longest]
        spots.append(tuple(where))
    return entries.at[spots[0]].set(low).at[spots[1]].set(top_value)


def steps_of(own_key, extent, cuts, low, high):
    def one(axis_at, parts):
        draws = jax.random.uniform(jax.random.fold_in(jax.random.fold_in(own_key, 6), axis_at), (parts,), jnp.float32, low / len(cuts), high / len(cuts))
        return jnp.repeat(jnp.exp(draws), extent[axis_at] // parts).reshape((-1,) + (1,) * (len(extent) - axis_at - 1))

    loudness = one(*cuts[0])
    for cut in cuts[1:]:
        loudness = loudness * one(*cut)
    return loudness


def noise(rng, shape, scale, limit, pieces=(), held_as=jnp.bfloat16):
    array = scale * jax.random.normal(rng, shape, jnp.float32)
    if pieces:
        array = array * steps_of(rng, shape, pieces, -0.22, 0.18)
    return jnp.clip(array, -limit, limit).astype(held_as)


def setup_inputs(seed: int = 0) -> dict:
    splits = jax.random.split(jax.random.key(seed), 7)
    features = noise(splits[0], (NX, NY, NZ, C), 1.0, 6.0, ((0, 8), (1, 4), (2, 4)))
    cotangent = noise(splits[1], (NX, NY, NZ, C), 1.0, 6.0, ((0, 8), (1, 4), (2, 4)))
    voxel_mask = place_ends((jax.random.randint(splits[2], (NX, NY, NZ), 0, 4) < 3).astype(jnp.int32), jax.random.fold_in(splits[2], 1), 0, 1)
    brick_active = place_ends((jax.random.randint(splits[3], (NX // BRICK, NY // BRICK, NZ // BRICK), 0, 4) < 3).astype(jnp.int32), jax.random.fold_in(splits[3], 1), 0, 1)
    first_weight = noise(splits[4], (27, C, C), (27 * C) ** -0.5, 0.109375)
    second_weight = noise(splits[5], (27, C, C), (27 * C) ** -0.5, 0.109375)
    return {"features": features, "cotangent": cotangent, "voxel_mask": voxel_mask, "brick_active": brick_active, "first_weight": first_weight, "second_weight": second_weight}


def tap_offsets():
    return [(number // 9, number // 3 % 3, number % 3) for number in range(27)]

def pad_grid(values):
    return jnp.pad(values, ((1, 1), (1, 1), (1, 1), (0, 0)))

def convolve(padded, weight, sizes):
    size_x, size_y, size_z = sizes
    accumulated = jnp.zeros((size_x * size_y * size_z, weight.shape[2]), jnp.float32)
    for number, (shift_x, shift_y, shift_z) in enumerate(tap_offsets()):
        portion = padded[shift_x:shift_x + size_x, shift_y:shift_y + size_y, shift_z:shift_z + size_z]
        portion = portion.reshape(-1, padded.shape[3])
        accumulated = accumulated + jnp.dot(portion, weight[number], preferred_element_type=jnp.float32)
    return accumulated.reshape(size_x, size_y, size_z, weight.shape[2])

def transposed(padded, weight, sizes):
    size_x, size_y, size_z = sizes
    accumulated = jnp.zeros((size_x * size_y * size_z, weight.shape[1]), jnp.float32)
    for number, (shift_x, shift_y, shift_z) in enumerate(tap_offsets()):
        start_x, start_y, start_z = (2 - shift_x, 2 - shift_y, 2 - shift_z)
        portion = padded[start_x:start_x + size_x, start_y:start_y + size_y, start_z:start_z + size_z]
        portion = portion.reshape(-1, padded.shape[3])
        accumulated = accumulated + jnp.dot(portion, weight[number].T, preferred_element_type=jnp.float32)
    return accumulated.reshape(size_x, size_y, size_z, weight.shape[1])

def kernel_grad(padded, upstream, sizes):
    size_x, size_y, size_z = sizes
    flat_up = upstream.reshape(-1, upstream.shape[3])
    results = []
    for number, (shift_x, shift_y, shift_z) in enumerate(tap_offsets()):
        portion = padded[shift_x:shift_x + size_x, shift_y:shift_y + size_y, shift_z:shift_z + size_z]
        portion = portion.reshape(-1, padded.shape[3])
        results.append(lax.dot_general(portion, flat_up, (((0,), (0,)), ((), ())), preferred_element_type=jnp.float32))
    return jnp.stack(results)

def reference(features, cotangent, voxel_mask, brick_active, first_weight, second_weight):
    grid_sizes = (NX, NY, NZ)
    bricks = jnp.repeat(jnp.repeat(jnp.repeat(brick_active, BRICK, 0), BRICK, 1), BRICK, 2)
    occupancy = (voxel_mask * bricks).astype(jnp.bfloat16)[..., None]
    mask_wide = occupancy.astype(jnp.float32)
    masked_in = features * occupancy
    first_pre = convolve(pad_grid(masked_in), first_weight, grid_sizes) * mask_wide
    hidden = jax.nn.silu(first_pre).astype(jnp.bfloat16)
    padded_hidden = pad_grid(hidden)
    output_field = (convolve(padded_hidden, second_weight, grid_sizes) * mask_wide).astype(jnp.bfloat16)
    upstream = cotangent * occupancy
    factor = 1.0 / math.sqrt(NX * NY * NZ)
    grad_second = kernel_grad(padded_hidden, upstream, grid_sizes) * factor
    back_hidden = transposed(pad_grid(upstream), second_weight, grid_sizes)
    sigmoid_part = jax.nn.sigmoid(first_pre)
    slope = sigmoid_part * (1.0 + first_pre * (1.0 - sigmoid_part))
    first_up = (back_hidden * slope * mask_wide).astype(jnp.bfloat16)
    grad_first = kernel_grad(pad_grid(masked_in), first_up, grid_sizes) * factor
    grad_features = (transposed(pad_grid(first_up), first_weight, grid_sizes) * mask_wide).astype(jnp.bfloat16)
    return (output_field, grad_features, grad_first, grad_second)
```

```python
import functools
import math

import jax
import jax.numpy as jnp
from jax import lax
from jax.experimental import pallas as pl
from jax.experimental.pallas import tpu as pltpu
from jax.sharding import PartitionSpec as P

BRICK = 8
AXES = ("gx", "gy", "gz")
BF = jnp.bfloat16
F32 = jnp.float32
VMEM = pl.BlockSpec(memory_space=pltpu.VMEM)
SMEM = pl.BlockSpec(memory_space=pltpu.SMEM)
MAIN_X = 512
MAIN_Y = 640
LIMIT = 60 * 1024 * 1024


def shape_of(shape, dtype):
    return jax.ShapeDtypeStruct(shape, dtype)


def weights_kernel(w1, w2, p1, p2, t1, t2):
    zero = jnp.zeros((128, 128), BF)

    def forward(src):
        return lambda t: src[t]

    def backward(src):
        return lambda t: src[26 - t].astype(F32).T.astype(BF)

    for out, get in ((p1, forward(w1)), (p2, forward(w2)), (t1, backward(w1)), (t2, backward(w2))):
        for b in range(3):
            for c in range(3):
                taps = [get(a * 9 + b * 3 + c) for a in range(3)]
                for s in range(4):
                    group, k = (s // 2) * 3 + b, (s % 2) * 384 + c * 128
                    out[group, k : k + 128, 0:128] = taps[s] if s < 3 else zero
                    out[group, k : k + 128, 128:256] = taps[s - 1] if s > 0 else zero


def prepare_weights(first_weight, second_weight):
    one = shape_of((6, 768, 256), BF)
    return pl.pallas_call(
        weights_kernel,
        out_shape=(one,) * 4,
        in_specs=[VMEM] * 2,
        out_specs=(VMEM,) * 4,
        compiler_params=pltpu.CompilerParams(vmem_limit_bytes=LIMIT),
        cost_estimate=pl.CostEstimate(flops=0, bytes_accessed=13_000_000, transcendentals=0),
        name="weights",
    )(first_weight, second_weight)


def gather_shifts(cat, rims, main, xm, xp, ym, yp, zm, zp):
    for arr in range(2):
        base = arr * 10
        cat[base + 1 : base + 9, 1:9, :, 128:256] = main[arr]
        for x, face in ((0, xm), (9, xp)):
            cat[base + x, 1:9, :, 128:256] = face[arr * 256 : arr * 256 + 256, :].reshape(8, 32, 128)
        for y, face in ((0, ym), (9, yp)):
            cat[base : base + 10, y, :, 128:256] = face[arr * 320 : arr * 320 + 320, :].reshape(10, 32, 128)
        for side, own in ((0, zm), (1, zp)):
            rims[side, base + 1 : base + 9, 1:9, :] = own[arr].astype(F32)
            for x, face in ((0, xm), (9, xp)):
                row = MAIN_X + side * 16 + arr * 8
                rims[side, base + x, 1:9, :] = face[row : row + 8, :].astype(F32)
            for y, face in ((0, ym), (9, yp)):
                row = MAIN_Y + side * 32 + arr * 16
                piece = face[row : row + 16, :].astype(F32)
                for x in range(10):
                    rims[side, base + x, y : y + 1, :] = piece[x : x + 1, :]
    place = lax.broadcasted_iota(jnp.int32, (32, 128), 0)

    def step(ax, _):
        for y in range(10):
            block = cat[ax, y, :, 128:256].astype(F32)
            below = jnp.where(place == 0, rims[0, ax, y : y + 1, :], pltpu.roll(block, 1, 0))
            above = jnp.where(place == 31, rims[1, ax, y : y + 1, :], pltpu.roll(block, 31, 0))
            cat[ax, y, :, 0:128] = below.astype(BF)
            cat[ax, y, :, 256:384] = above.astype(BF)
        return 0

    lax.fori_loop(0, 20, step, 0)


def convolve(cat, arr, weight, emit):
    def step(pair, _):
        x0 = pair * 2
        total = jnp.zeros((256, 256), F32)
        for half in range(2):
            for b in range(3):
                slabs = [
                    cat[arr * 10 + x0 + half * 2 + s, b : b + 8].reshape(256, 384) for s in range(2)
                ]
                total = total + jnp.dot(
                    jnp.concatenate(slabs, axis=1), weight[half * 3 + b], preferred_element_type=F32
                )
        emit(x0, total[:, 0:128])
        emit(x0 + 1, total[:, 128:256])
        return 0

    lax.fori_loop(0, 4, step, 0)


def first_kernel(
    where, main, xm, xp, ym, yp, zm, zp, occ, p1, t2,
    fields, keep, send,
    cat, rims, slope, hid_t, up_t,
):
    gather_shifts(cat, rims, main, xm, xp, ym, yp, zm, zp)

    def emit_first(x, total):
        mask = occ[x].reshape(256, 128).astype(F32)
        value = total * mask
        gate = jax.nn.sigmoid(value)
        hidden = value * gate
        slope[x] = gate * (1.0 + value * (1.0 - gate)) * mask
        fields[0, x] = hidden.astype(BF).reshape(8, 32, 128)
        hid_t[:, pl.ds(pl.multiple_of(x * 256, 256), 256)] = hidden.T.astype(BF)

    convolve(cat, 0, p1, emit_first)

    def emit_up(x, total):
        value = total * slope[x]
        fields[1, x] = value.astype(BF).reshape(8, 32, 128)
        up_t[:, pl.ds(pl.multiple_of(x * 256, 256), 256)] = value.T.astype(BF)

    convolve(cat, 1, t2, emit_up)

    core = where[0]

    def grads(number, _):
        a, b = number // 3, number % 3
        columns = pl.ds(pl.multiple_of(number * 384, 128), 384)
        first = jnp.dot(
            up_t[...],
            cat[pl.ds(a, 8), pl.ds(b, 8)].reshape(2048, 384),
            preferred_element_type=F32,
        )
        second = jnp.dot(
            hid_t[...],
            cat[pl.ds(10 + a, 8), pl.ds(b, 8)].reshape(2048, 384),
            preferred_element_type=F32,
        )
        second = jnp.concatenate(
            [second[h * 64 + y * 16 : h * 64 + y * 16 + 16] for y in range(4) for h in range(2)], axis=0
        )

        @pl.when(core == 0)
        def _():
            keep[:, :, columns] = first.reshape(4, 32, 384)
            send[:, :, columns] = second.astype(BF).reshape(4, 32, 384)

        @pl.when(core == 1)
        def _():
            keep[:, :, columns] = second.reshape(4, 32, 384)
            send[:, :, columns] = first.astype(BF).reshape(4, 32, 384)

        return 0

    lax.fori_loop(0, 9, grads, 0)


def first_pass(where, main, halos, occ, p1, t2):
    return pl.pallas_call(
        first_kernel,
        out_shape=(
            shape_of((2, 8, 8, 32, 128), BF),
            shape_of((4, 32, 27 * 128), F32),
            shape_of((4, 32, 27 * 128), BF),
        ),
        in_specs=[SMEM] + [VMEM] * 10,
        out_specs=(VMEM,) * 3,
        scratch_shapes=[
            pltpu.VMEM((20, 10, 32, 384), BF),
            pltpu.VMEM((2, 20, 16, 128), F32),
            pltpu.VMEM((8, 256, 128), F32),
            pltpu.VMEM((128, 2048), BF),
            pltpu.VMEM((128, 2048), BF),
        ],
        compiler_params=pltpu.CompilerParams(vmem_limit_bytes=LIMIT),
        cost_estimate=pl.CostEstimate(flops=8_000_000_000, bytes_accessed=12_000_000, transcendentals=262144),
        name="first_pass",
    )(where, main, *halos, occ, p1, t2)


def second_kernel(main, xm, xp, ym, yp, zm, zp, occ, p2, t1, out, grad, cat, rims):
    gather_shifts(cat, rims, main, xm, xp, ym, yp, zm, zp)

    def emit_to(target):
        def emit(x, total):
            mask = occ[x].reshape(256, 128).astype(F32)
            target[x] = (total * mask).astype(BF).reshape(8, 32, 128)

        return emit

    convolve(cat, 0, p2, emit_to(out))
    convolve(cat, 1, t1, emit_to(grad))


def second_pass(main, halos, occ, p2, t1):
    return pl.pallas_call(
        second_kernel,
        out_shape=(shape_of((8, 8, 32, 128), BF),) * 2,
        in_specs=[VMEM] * 10,
        out_specs=(VMEM,) * 2,
        scratch_shapes=[
            pltpu.VMEM((20, 10, 32, 384), BF),
            pltpu.VMEM((2, 20, 16, 128), F32),
        ],
        compiler_params=pltpu.CompilerParams(vmem_limit_bytes=LIMIT),
        cost_estimate=pl.CostEstimate(flops=4_000_000_000, bytes_accessed=8_000_000, transcendentals=0),
        name="second_pass",
    )(main, *halos, occ, p2, t1)


def neighbour(values, axis, step):
    count = lax.axis_size(axis)
    return lax.ppermute(
        values, axis, [(i, i + step) for i in range(count) if 0 <= i + step < count]
    )


def exchange(main):
    zm = neighbour(main[:, :, :, 31], "gz", 1)
    zp = neighbour(main[:, :, :, 0], "gz", -1)

    def x_face(x):
        return jnp.concatenate(
            [main[:, x].reshape(512, 128), zm[:, x].reshape(16, 128), zp[:, x].reshape(16, 128)]
        )

    xm = neighbour(x_face(7), "gx", 1)
    xp = neighbour(x_face(0), "gx", -1)

    def y_face(y):
        inner = jnp.concatenate(
            [
                xm[:MAIN_X].reshape(2, 1, 8, 32, 128)[:, :, y],
                main[:, :, y],
                xp[:MAIN_X].reshape(2, 1, 8, 32, 128)[:, :, y],
            ],
            axis=1,
        ).reshape(MAIN_Y, 128)
        rims = jnp.concatenate(
            [
                xm[MAIN_X:].reshape(2, 2, 1, 8, 128)[:, :, :, y],
                jnp.stack([zm[:, :, y], zp[:, :, y]]),
                xp[MAIN_X:].reshape(2, 2, 1, 8, 128)[:, :, :, y],
                jnp.zeros((2, 2, 6, 128), BF),
            ],
            axis=2,
        ).reshape(64, 128)
        return jnp.concatenate([inner, rims])

    ym = neighbour(y_face(7), "gy", 1)
    yp = neighbour(y_face(0), "gy", -1)
    return xm, xp, ym, yp, zm, zp


def device_places():
    places = []
    for number in range(128):
        gx, gy, gz = number // 16, number // 4 % 4, number % 4
        places.append(((gx // 4) * 2 + gz // 2, gx % 4, gy, gz % 2))
    return places


def permute_chips(values, move):
    places = device_places()
    index = {place: number for number, place in enumerate(places)}
    return lax.ppermute(values, AXES, [(n, index[move(*place)]) for n, place in enumerate(places)])


def swap_cores(values):
    return permute_chips(values, lambda x, y, z, c: (x, y, z, 1 - c))


def along_rows(step):
    return lambda x, y, z, c: (x, (y + step * c) % 4, (z + step * (1 - c)) % 4, c)


def along_lanes(step):
    return lambda x, y, z, c: (x, (y + step * (1 - c)) % 4, (z + step * c) % 4, c)


def along_x(step):
    return lambda x, y, z, c: ((x + step) % 4, y, z, c)


def split_kernel(picks, keep, got, own, m1, m2, m3):
    def block(i):
        return keep[picks[i]] + got[picks[i]].astype(F32)

    own[...] = block(0)
    for i, out in ((1, m1), (2, m2), (3, m3)):
        out[...] = block(i).astype(BF)


def split_rows(picks, keep, got):
    rows, lanes = keep.shape[1:]
    return pl.pallas_call(
        split_kernel,
        out_shape=(shape_of((rows, lanes), F32),) + (shape_of((rows, lanes), BF),) * 3,
        in_specs=[SMEM, VMEM, VMEM],
        out_specs=(VMEM,) * 4,
        cost_estimate=pl.CostEstimate(flops=0, bytes_accessed=5_000_000, transcendentals=0),
        name="split_rows",
    )(picks, keep, got)


def halves_kernel(picks, own, r1, r2, r3, kept, m1, m2, m3):
    total = own[...] + (r1[...].astype(F32) + r2[...].astype(F32)) + r3[...].astype(F32)
    parts = (total[0:16], total[16:32])
    for i, out in ((0, kept), (1, m1), (2, m2), (3, m3)):
        for h in range(2):

            @pl.when(picks[i] == h)
            def _():
                out[...] = parts[h].astype(out.dtype)


def split_halves(picks, own, parts):
    lanes = own.shape[1]
    return pl.pallas_call(
        halves_kernel,
        out_shape=(shape_of((16, lanes), F32),) + (shape_of((16, lanes), BF),) * 3,
        in_specs=[SMEM] + [VMEM] * 4,
        out_specs=(VMEM,) * 4,
        cost_estimate=pl.CostEstimate(flops=0, bytes_accessed=1_500_000, transcendentals=0),
        name="split_halves",
    )(picks, own, *parts)


def sum_kernel(own, r1, r2, r3, total, message):
    value = own[...] + (r1[...].astype(F32) + r2[...].astype(F32)) + r3[...].astype(F32)
    total[...] = value
    message[...] = value.astype(BF)


def sum_parts(own, parts):
    return pl.pallas_call(
        sum_kernel,
        out_shape=(shape_of(own.shape, F32), shape_of(own.shape, BF)),
        in_specs=[VMEM] * 4,
        out_specs=(VMEM,) * 2,
        cost_estimate=pl.CostEstimate(flops=0, bytes_accessed=1_000_000, transcendentals=0),
        name="sum_parts",
    )(own, *parts)


def reduce_grads(keep, send, factor):
    gx, gy, gz = (lax.axis_index(name) for name in AXES)
    x, y, z, core = (gx // 4) * 2 + gz // 2, gx % 4, gy, gz % 2
    steps = jnp.arange(4)
    got = swap_cores(send)
    blocks = (jnp.where(core == 0, z, y) + steps) % 4
    own, *messages = split_rows(blocks.astype(jnp.int32), keep, got)
    parts = [permute_chips(m, along_rows(i + 1)) for i, m in enumerate(messages)]
    targets = (x + steps) % 4
    halves = jnp.where(core == 0, targets % 2, targets // 2)
    own, *messages = split_halves(halves.astype(jnp.int32), own, parts)
    parts = [permute_chips(m, along_x(i + 1)) for i, m in enumerate(messages)]
    own, message = sum_parts(own, parts)
    parts = [permute_chips(message, along_lanes(i + 1)) for i in range(3)]
    total, _ = sum_parts(own, parts)
    lane = jnp.where(core == 0, gx, z * 2 + gz // 2) * 16
    piece = lax.dynamic_slice_in_dim(total.reshape(16, 27, 128), lane, 16, axis=2) * factor
    other = swap_cores(piece)
    first = jnp.where(core == 0, piece, other)
    second = jnp.where(core == 0, other, piece)
    first = lax.dynamic_slice_in_dim(first, core * 8, 8, axis=0)
    second = lax.dynamic_slice_in_dim(second, core * 8, 8, axis=2)
    return jnp.transpose(first, (1, 2, 0)), jnp.transpose(second, (1, 0, 2))[::-1]


def on_device(features, cotangent, voxel_mask, brick_active, first_weight, second_weight):
    total_voxels = voxel_mask.size * 128
    factor = 1.0 / math.sqrt(total_voxels)
    bricks = jnp.repeat(jnp.repeat(jnp.repeat(brick_active, BRICK, 0), BRICK, 1), BRICK, 2)
    occupancy = (voxel_mask * bricks).astype(BF)[..., None]
    occ = jnp.broadcast_to(occupancy, features.shape)
    main = jnp.stack([features * occupancy, cotangent * occupancy])
    p1, p2, t1, t2 = prepare_weights(first_weight, second_weight)
    where = (lax.axis_index("gz") % 2).astype(jnp.int32)[None]
    fields, keep, send = first_pass(where, main, exchange(main), occ, p1, t2)
    grad_first, grad_second = reduce_grads(keep, send, factor)
    output_field, grad_features = second_pass(fields, exchange(fields), occ, p2, t1)
    return (output_field, grad_features, grad_first, grad_second)


def solution(mesh):
    return jax.shard_map(
        on_device,
        mesh=mesh,
        in_specs=(
            P("gx", "gy", "gz", None),
            P("gx", "gy", "gz", None),
            P("gx", "gy", "gz"),
            P("gx", "gy", "gz"),
            P(),
            P(),
        ),
        out_specs=(
            P("gx", "gy", "gz", None),
            P("gx", "gy", "gz", None),
            P(None, "gx", ("gy", "gz")),
            P(None, "gx", ("gy", "gz")),
        ),
        check_vma=False,
    )
```

```python
import functools
import math

import jax
import jax.numpy as jnp
from jax import lax
from jax.experimental import pallas as pl
from jax.experimental.pallas import tpu as pltpu
from jax.sharding import PartitionSpec as P


BRICK = 8
AXES = ("gx", "gy", "gz")
BF = jnp.bfloat16
F32 = jnp.float32
VMEM = pl.BlockSpec(memory_space=pltpu.VMEM)
SMEM = pl.BlockSpec(memory_space=pltpu.SMEM)
X, Y, Z = 0, 1, 2
FACE = 512
MIB = 1024 * 1024


def shape_of(shape, dtype):
    return jax.ShapeDtypeStruct(shape, dtype)


def weights_kernel(wp, wt, pairs, flipped):
    zero = jnp.zeros((128, 128), BF)

    def forward(t):
        return wp[t]

    def backward(t):
        return wt[26 - t].astype(F32).T.astype(BF)

    for out, get in ((pairs, forward), (flipped, backward)):
        for b in range(3):
            for c in range(3):
                taps = [get(a * 9 + b * 3 + c) for a in range(3)]
                for s in range(4):
                    group, k = (s // 2) * 3 + b, (s % 2) * 384 + c * 128
                    out[group, k : k + 128, 0:128] = taps[s] if s < 3 else zero
                    out[group, k : k + 128, 128:256] = taps[s - 1] if s > 0 else zero


def prepare_weights(paired, turned):
    one = shape_of((6, 768, 256), BF)
    return pl.pallas_call(
        weights_kernel,
        out_shape=(one,) * 2,
        in_specs=[VMEM] * 2,
        out_specs=(VMEM,) * 2,
        compiler_params=pltpu.CompilerParams(vmem_limit_bytes=12 * MIB),
        cost_estimate=pl.CostEstimate(flops=0, bytes_accessed=6_500_000, transcendentals=0),
        name="weights",
    )(paired, turned)


def place_on(axis):
    at = lax.axis_index(AXES[axis])
    return at, at & 1, (at != 0) & (at != lax.axis_size(AXES[axis]) - 1)


def chip_place():
    gx, gy, gz = (lax.axis_index(name) for name in AXES)
    return (gx >> 2) * 2 + (gz >> 1), gx & 3, gy, gz & 1


def gather_shifts(cat, rims, arrays, main, x0, x1, y0, y1, z0, z1):
    odd = [place_on(axis)[1] for axis in range(3)]
    inner = [place_on(axis)[2] for axis in range(3)]
    spots = {X: 9 - 9 * odd[X], X + 10: 9 * odd[X], Y: 9 - 9 * odd[Y], Y + 10: 9 * odd[Y]}

    def kept(values, *axes):
        for axis in axes:
            values = jnp.where(inner[axis], values, jnp.zeros_like(values))
        return values

    for at, arr in enumerate(arrays):
        base = at * 10
        cat[base + 1 : base + 9, 1:9, :, 128:256] = main[arr]
        for slot, face in ((0, x0), (1, x1)):
            part = face[arr * 256 : arr * 256 + 256, :]
            part = kept(part, X) if slot else part
            cat[base + spots[X + 10 * slot], 1:9, :, 128:256] = part.reshape(8, 32, 128)
        for slot, face in ((0, y0), (1, y1)):
            ends = (Y,) if slot else ()
            y = spots[Y + 10 * slot]
            part = kept(face[arr * 256 : arr * 256 + 256, :], *ends)
            cat[base + 1 : base + 9, y, :, 128:256] = part.reshape(8, 32, 128)
            for side in range(2):
                row = FACE + side * 64 + arr * 32
                part = kept(face[row : row + 32, :], *ends, *((X,) if side else ()))
                cat[base + spots[X + 10 * side], y, :, 128:256] = part
        for slot, own in ((0, z0), (1, z1)):
            last = (Z,) if slot else ()
            rims[slot, base + 1 : base + 9, 1:9, :] = kept(own[arr].astype(F32), *last)
            for side, face in ((0, x0), (1, x1)):
                row = FACE + slot * 16 + arr * 8
                part = kept(face[row : row + 8, :].astype(F32), *last, *((X,) if side else ()))
                rims[slot, base + spots[X + 10 * side], 1:9, :] = part
            for side, face in ((0, y0), (1, y1)):
                row = FACE + 128 + slot * 32 + arr * 16
                part = kept(face[row : row + 16, :].astype(F32), *last, *((Y,) if side else ()))
                y = pl.ds(spots[Y + 10 * side], 1)
                rims[slot, base + spots[X], y, :] = part[0:1, :]
                rims[slot, base + spots[X + 10], y, :] = kept(part[9:10, :], X)
                for x in range(1, 9):
                    rims[slot, base + x, y, :] = part[x : x + 1, :]
    place = lax.broadcasted_iota(jnp.int32, (32, 128), 0)
    before, after = 1 - odd[Z], odd[Z]

    def step(ax, _):
        for y in range(10):
            block = cat[ax, y, :, 128:256].astype(F32)
            below = jnp.where(place == 0, rims[before, ax, y : y + 1, :], pltpu.roll(block, 1, 0))
            above = jnp.where(place == 31, rims[after, ax, y : y + 1, :], pltpu.roll(block, 31, 0))
            cat[ax, y, :, 0:128] = below.astype(BF)
            cat[ax, y, :, 256:384] = above.astype(BF)
        return 0

    lax.fori_loop(0, 10 * len(arrays), step, 0)


def convolve(cat, arr, weight, emit):
    def step(pair, _):
        x0 = pair * 2
        total = jnp.zeros((256, 256), F32)
        for half in range(2):
            for b in range(3):
                slabs = [
                    cat[arr * 10 + x0 + half * 2 + s, b : b + 8].reshape(256, 384) for s in range(2)
                ]
                total = total + jnp.dot(
                    jnp.concatenate(slabs, axis=1), weight[half * 3 + b], preferred_element_type=F32
                )
        emit(x0, total[:, 0:128])
        emit(x0 + 1, total[:, 128:256])
        return 0

    lax.fori_loop(0, 4, step, 0)


def first_kernel(
    main, x0, x1, y0, y1, z0, z1, occ, p1, t2,
    fields, keep, send, q0, q1,
    cat, rims, slope, hid_t, up_t, rows,
):
    gather_shifts(cat, rims, (0, 1), main, x0, x1, y0, y1, z0, z1)

    def emit_first(x, total):
        mask = occ[x].reshape(256, 128).astype(F32)
        value = total * mask
        gate = jax.nn.sigmoid(value)
        hidden = value * gate
        slope[x] = gate * (1.0 + value * (1.0 - gate)) * mask
        fields[0, x] = hidden.astype(BF).reshape(8, 32, 128)
        hid_t[:, pl.ds(pl.multiple_of(x * 256, 256), 256)] = hidden.T.astype(BF)
        z_faces(0, x, hidden, rows, q0, q1)

    convolve(cat, 0, p1, emit_first)

    def emit_up(x, total):
        value = total * slope[x]
        fields[1, x] = value.astype(BF).reshape(8, 32, 128)
        up_t[:, pl.ds(pl.multiple_of(x * 256, 256), 256)] = value.T.astype(BF)
        z_faces(1, x, value, rows, q0, q1)

    convolve(cat, 1, t2, emit_up)

    core = chip_place()[3]

    def grads(number, _):
        a, b = number // 3, number % 3
        columns = pl.ds(pl.multiple_of(number * 384, 128), 384)
        first = jnp.dot(
            up_t[...],
            cat[pl.ds(a, 8), pl.ds(b, 8)].reshape(2048, 384),
            preferred_element_type=F32,
        )
        second = jnp.dot(
            hid_t[...],
            cat[pl.ds(10 + a, 8), pl.ds(b, 8)].reshape(2048, 384),
            preferred_element_type=F32,
        )
        second = jnp.concatenate(
            [second[h * 64 + y * 16 : h * 64 + y * 16 + 16] for y in range(4) for h in range(2)], axis=0
        )

        @pl.when(core == 0)
        def _():
            keep[:, :, columns] = first.reshape(4, 32, 384)
            send[:, :, columns] = second.astype(BF).reshape(4, 32, 384)

        @pl.when(core == 1)
        def _():
            keep[:, :, columns] = second.reshape(4, 32, 384)
            send[:, :, columns] = first.astype(BF).reshape(4, 32, 384)

        return 0

    lax.fori_loop(0, 9, grads, 0)


def first_pass(main, halos, occ, p1, t2):
    return pl.pallas_call(
        first_kernel,
        out_shape=(
            shape_of((2, 8, 8, 32, 128), BF),
            shape_of((4, 32, 27 * 128), F32),
            shape_of((4, 32, 27 * 128), BF),
            shape_of((2, 8, 8, 128), BF),
            shape_of((2, 8, 8, 128), BF),
        ),
        in_specs=[VMEM] * 10,
        out_specs=(VMEM,) * 5,
        scratch_shapes=[
            pltpu.VMEM((20, 10, 32, 384), BF),
            pltpu.VMEM((2, 20, 16, 128), F32),
            pltpu.VMEM((8, 256, 128), F32),
            pltpu.VMEM((128, 2048), BF),
            pltpu.VMEM((128, 2048), BF),
            pltpu.VMEM((256, 128), F32),
        ],
        compiler_params=pltpu.CompilerParams(vmem_limit_bytes=16 * MIB),
        cost_estimate=pl.CostEstimate(flops=8_000_000_000, bytes_accessed=12_000_000, transcendentals=262144),
        name="first_pass",
    )(main, *halos, occ, p1, t2)


def second_kernel(arr, main, x0, x1, y0, y1, z0, z1, occ, weight, out, cat, rims):
    gather_shifts(cat, rims, (arr,), main, x0, x1, y0, y1, z0, z1)

    def emit(x, total):
        mask = occ[x].reshape(256, 128).astype(F32)
        out[x] = (total * mask).astype(BF).reshape(8, 32, 128)

    convolve(cat, 0, weight, emit)


def second_pass(arr, main, halos, occ, weight):
    return pl.pallas_call(
        functools.partial(second_kernel, arr),
        out_shape=shape_of((8, 8, 32, 128), BF),
        in_specs=[VMEM] * 9,
        out_specs=VMEM,
        scratch_shapes=[
            pltpu.VMEM((10, 10, 32, 384), BF),
            pltpu.VMEM((2, 10, 16, 128), F32),
        ],
        compiler_params=pltpu.CompilerParams(vmem_limit_bytes=10 * MIB),
        cost_estimate=pl.CostEstimate(flops=2_000_000_000, bytes_accessed=4_000_000, transcendentals=0),
        name="second_pass",
    )(main, *halos, occ, weight)


def swap_faces(values, axis, slot):
    count = lax.axis_size(axis)
    pairs = [(i, i ^ 1 if slot == 0 else (i - 1 + 2 * (i % 2)) % count) for i in range(count)]
    return lax.ppermute(values, axis, pairs)


def small_call(kernel, out_shape, operands, scratch=(), limit=2, inputs=None):
    single = not isinstance(out_shape, tuple)
    total = sum(v.size * v.dtype.itemsize for v in operands)
    return pl.pallas_call(
        kernel,
        out_shape=out_shape,
        in_specs=inputs or [VMEM] * len(operands),
        out_specs=VMEM if single else (VMEM,) * len(out_shape),
        scratch_shapes=scratch,
        compiler_params=pltpu.CompilerParams(vmem_limit_bytes=limit * MIB),
        cost_estimate=pl.CostEstimate(flops=0, bytes_accessed=total, transcendentals=0),
    )(*operands)


def z_faces(arr, x, values, rows, m0, m1):
    odd = place_on(Z)[1]
    rows[...] = values
    m0[arr, x] = rows[pl.ds(31 - 31 * odd, 8, stride=32), :].astype(BF)
    m1[arr, x] = rows[pl.ds(31 * odd, 8, stride=32), :].astype(BF)


def mask_kernel(bricks, features, cotangent, mask, main, occ, m0, m1, rows):
    lane = lax.broadcasted_iota(jnp.int32, (8, 32), 1)
    active = jnp.zeros((8, 32), jnp.int32)
    for k in range(4):
        active = jnp.where(lane // BRICK == k, bricks[0, 0, k], active)
    diagonal = lax.broadcasted_iota(jnp.int32, (32, 32), 0) == lax.broadcasted_iota(jnp.int32, (32, 32), 1)
    ones = jnp.ones((32, 128), BF)
    for x in range(8):
        flags = (mask[x] * active).astype(F32)
        spread = [
            jnp.where(diagonal, jnp.broadcast_to(flags[y : y + 1], (32, 32)), 0.0) for y in range(8)
        ]
        wide = jnp.dot(jnp.concatenate(spread).astype(BF), ones, preferred_element_type=F32)
        occ[x] = wide.astype(BF).reshape(8, 32, 128)
        for arr, source in ((0, features), (1, cotangent)):
            masked = source[x].reshape(256, 128).astype(F32) * wide
            main[arr, x] = masked.astype(BF).reshape(8, 32, 128)
            z_faces(arr, x, masked, rows, m0, m1)


def mask_inputs(features, cotangent, voxel_mask, brick_active):
    z_message = shape_of((2, 8, 8, 128), BF)
    return small_call(
        mask_kernel,
        (shape_of((2, 8, 8, 32, 128), BF), shape_of((8, 8, 32, 128), BF), z_message, z_message),
        (brick_active, features, cotangent, voxel_mask),
        scratch=[pltpu.VMEM((256, 128), F32)],
        limit=4,
        inputs=[SMEM] + [VMEM] * 3,
    )


def x_kernel(main, z0, z1, m0, m1):
    odd = place_on(X)[1]
    for out, x in ((m0, 7 - 7 * odd), (m1, 7 * odd)):
        for arr in range(2):
            out[arr * 256 : arr * 256 + 256, :] = main[arr, x].reshape(256, 128)
            for slot, rims in ((0, z0), (1, z1)):
                row = FACE + slot * 16 + arr * 8
                out[row : row + 8, :] = rims[arr, x]


def y_kernel(main, x0, x1, z0, z1, m0, m1, ends, own, piece):
    odd = place_on(Y)[1]
    piece[...] = jnp.zeros_like(piece)
    for side, face in ((0, x0), (1, x1)):
        ends[side] = face[FACE : FACE + 32, :].astype(F32)
    for slot, rims in ((0, z0), (1, z1)):
        own[slot] = rims[...].astype(F32).reshape(128, 128)
    for out, y in ((m0, 7 - 7 * odd), (m1, 7 * odd)):
        for arr in range(2):
            out[arr * 256 : arr * 256 + 256, :] = main[arr, :, y].reshape(256, 128)
            for side, face in ((0, x0), (1, x1)):
                row = FACE + side * 64 + arr * 32
                from_row = pl.multiple_of(arr * 256 + y * 32, 32)
                out[row : row + 32, :] = face[pl.ds(from_row, 32), :]
            for slot in range(2):
                at = slot * 16 + arr * 8
                piece[0:1, :] = ends[0, pl.ds(at + y, 1), :]
                piece[1:9, :] = own[slot, pl.ds(arr * 64 + y, 8, stride=8), :]
                piece[9:10, :] = ends[1, pl.ds(at + y, 1), :]
                row = FACE + 128 + slot * 32 + arr * 16
                out[row : row + 16, :] = piece[...].astype(BF)


def exchange(main, messages):
    z0 = swap_faces(messages[0], "gz", 0)
    z1 = swap_faces(messages[1], "gz", 1)
    messages = small_call(x_kernel, (shape_of((544, 128), BF),) * 2, (main, z0, z1))
    x0 = swap_faces(messages[0], "gx", 0)
    x1 = swap_faces(messages[1], "gx", 1)
    messages = small_call(
        y_kernel,
        (shape_of((704, 128), BF),) * 2,
        (main, x0, x1, z0, z1),
        scratch=[
            pltpu.VMEM((2, 32, 128), F32),
            pltpu.VMEM((2, 128, 128), F32),
            pltpu.VMEM((16, 128), F32),
        ],
    )
    y0 = swap_faces(messages[0], "gy", 0)
    y1 = swap_faces(messages[1], "gy", 1)
    return x0, x1, y0, y1, z0, z1


def device_places():
    places = []
    for number in range(128):
        gx, gy, gz = number // 16, number // 4 % 4, number % 4
        places.append(((gx // 4) * 2 + gz // 2, gx % 4, gy, gz % 2))
    return places


def permute_chips(values, move):
    places = device_places()
    index = {place: number for number, place in enumerate(places)}
    pairs = [(n, index[move(*place)]) for n, place in enumerate(places)]
    return lax.ppermute(values, AXES, pairs)


def swap_cores(values):
    return permute_chips(values, lambda x, y, z, c: (x, y, z, 1 - c))


PARTNERS = (1, 3, 2)


def along_rows(flip):
    return lambda x, y, z, c: (x, y ^ (flip * c), z ^ (flip * (1 - c)), c)


def along_lanes(flip):
    return lambda x, y, z, c: (x, y ^ (flip * (1 - c)), z ^ (flip * c), c)


def along_x(flip):
    return lambda x, y, z, c: (x ^ flip, y, z, c)


def split_kernel(keep, got, own, m1, m2, m3):
    _, y, z, core = chip_place()
    block = jnp.where(core == 0, z, y)
    for flip, out in zip((0,) + PARTNERS, (own, m1, m2, m3)):
        at = block ^ flip
        out[...] = (keep[at] + got[at].astype(F32)).astype(out.dtype)


def total_of(own, parts):
    r1, r2, r3 = (part[...].astype(F32) for part in parts)
    return own[...] + (r1 + r2) + r3


def halves_kernel(own, r1, r2, r3, kept, m1, m2, m3, whole):
    x, _, _, core = chip_place()
    whole[...] = total_of(own, (r1, r2, r3))
    for flip, out in zip((0,) + PARTNERS, (kept, m1, m2, m3)):
        chip = x ^ flip
        half = jnp.where(core == 0, chip & 1, chip >> 1)
        out[...] = whole[pl.ds(pl.multiple_of(half * 16, 16), 16), :].astype(out.dtype)


def sum_kernel(own, r1, r2, r3, total, message):
    value = total_of(own, (r1, r2, r3))
    total[...] = value
    message[...] = value.astype(BF)


def piece_kernel(factor, own, r1, r2, r3, piece):
    x, y, z, core = chip_place()
    block = jnp.where(core == 0, (x >> 1) * 4 + y, z * 2 + (x & 1))
    value = total_of(own, (r1, r2, r3)) * factor
    shift = (128 - block * 16) & 127
    for tap in range(27):
        at = jnp.where(core == 0, tap, 26 - tap)
        piece[at] = pltpu.roll(value[:, tap * 128 : tap * 128 + 128], shift, 1)
    for tap in range(27, 32):
        piece[tap] = jnp.zeros((16, 128), F32)


def outputs_kernel(mine, other, first, second, both):
    core = chip_place()[3]
    both[core] = mine[...].reshape(512, 128)
    both[1 - core] = other[...].reshape(512, 128)
    for j in range(8):
        turned = both[0, pl.ds(core * 8 + j, 32, stride=16), :].T
        first[pl.ds(j, 16, stride=8), :] = turned[0:16, :]
    for i in range(16):
        turned = both[1, pl.ds(i, 32, stride=16), :].T
        second[i * 8 : i * 8 + 8, :] = jnp.where(core == 0, turned[0:8, :], turned[8:16, :])


def reduce_grads(keep, send, factor):
    lanes = 27 * 128
    wide, thin = shape_of((32, lanes), BF), shape_of((16, lanes), BF)
    got = swap_cores(send)
    own, *messages = small_call(
        split_kernel, (shape_of((32, lanes), F32), wide, wide, wide), (keep, got)
    )
    parts = [permute_chips(m, along_rows(PARTNERS[i])) for i, m in enumerate(messages)]
    own, *messages = small_call(
        halves_kernel,
        (shape_of((16, lanes), F32), thin, thin, thin),
        (own, *parts),
        scratch=[pltpu.VMEM((32, lanes), F32)],
    )
    parts = [permute_chips(m, along_x(PARTNERS[i])) for i, m in enumerate(messages)]
    own, message = small_call(sum_kernel, (shape_of((16, lanes), F32), thin), (own, *parts))
    parts = [permute_chips(message, along_lanes(PARTNERS[i])) for i in range(3)]
    piece = small_call(
        functools.partial(piece_kernel, factor), shape_of((32, 16, 128), F32), (own, *parts)
    )
    other = swap_cores(piece)
    first, second = small_call(
        outputs_kernel,
        (shape_of((128, 32), F32),) * 2,
        (piece, other),
        scratch=[pltpu.VMEM((2, 512, 128), F32)],
    )
    return tuple(jnp.transpose(g.reshape(16, 8, 32)[:, :, :27], (2, 0, 1)) for g in (first, second))


def on_device(features, cotangent, voxel_mask, brick_active, first_weight, second_weight):
    factor = 1.0 / math.sqrt(voxel_mask.size * 128)
    main, occ, *faces = mask_inputs(features, cotangent, voxel_mask, brick_active)
    p1, t2 = prepare_weights(first_weight, second_weight)
    p2, t1 = prepare_weights(second_weight, first_weight)
    fields, keep, send, *next_faces = first_pass(main, exchange(main, faces), occ, p1, t2)
    halos = exchange(fields, next_faces)
    grad_first, grad_second = reduce_grads(keep, send, factor)
    output_field = second_pass(0, fields, halos, occ, p2)
    grad_features = second_pass(1, fields, halos, occ, t1)
    return (output_field, grad_features, grad_first, grad_second)


def solution(mesh):
    return jax.shard_map(
        on_device,
        mesh=mesh,
        in_specs=(
            P("gx", "gy", "gz", None),
            P("gx", "gy", "gz", None),
            P("gx", "gy", "gz"),
            P("gx", "gy", "gz"),
            P(),
            P(),
        ),
        out_specs=(
            P("gx", "gy", "gz", None),
            P("gx", "gy", "gz", None),
            P(None, "gx", ("gy", "gz")),
            P(None, "gx", ("gy", "gz")),
        ),
        check_vma=False,
    )
```

```python
import functools
import math

import jax
import jax.numpy as jnp
from jax import lax
from jax.experimental import pallas as pl
from jax.experimental.pallas import tpu as pltpu
from jax.sharding import PartitionSpec as P


BRICK = 8
AXES = ("gx", "gy", "gz")
BF = jnp.bfloat16
F32 = jnp.float32
VMEM = pl.BlockSpec(memory_space=pltpu.VMEM)
SMEM = pl.BlockSpec(memory_space=pltpu.SMEM)
X, Y, Z = 0, 1, 2
FACE = 512
MIB = 1024 * 1024


def shape_of(shape, dtype):
    return jax.ShapeDtypeStruct(shape, dtype)


def weights_kernel(wp, wt, pairs, flipped):
    zero = jnp.zeros((128, 128), BF)

    def forward(t):
        return wp[t]

    def backward(t):
        return wt[26 - t].astype(F32).T.astype(BF)

    for out, get in ((pairs, forward), (flipped, backward)):
        for b in range(3):
            for c in range(3):
                taps = [get(a * 9 + b * 3 + c) for a in range(3)]
                for s in range(4):
                    group, k = (s // 2) * 3 + b, (s % 2) * 384 + c * 128
                    out[group, k : k + 128, 0:128] = taps[s] if s < 3 else zero
                    out[group, k : k + 128, 128:256] = taps[s - 1] if s > 0 else zero


def prepare_weights(paired, turned):
    one = shape_of((6, 768, 256), BF)
    return pl.pallas_call(
        weights_kernel,
        out_shape=(one,) * 2,
        in_specs=[VMEM] * 2,
        out_specs=(VMEM,) * 2,
        compiler_params=pltpu.CompilerParams(vmem_limit_bytes=12 * MIB),
        cost_estimate=pl.CostEstimate(flops=0, bytes_accessed=6_500_000, transcendentals=0),
        name="weights",
    )(paired, turned)


def place_on(axis):
    at = lax.axis_index(AXES[axis])
    return at, at & 1, (at != 0) & (at != lax.axis_size(AXES[axis]) - 1)


def chip_place():
    gx, gy, gz = (lax.axis_index(name) for name in AXES)
    return (gx >> 2) * 2 + (gz >> 1), gx & 3, gy, gz & 1


class Places:
    def __init__(self):
        self.odd, self.inner = zip(*(place_on(axis)[1:] for axis in range(3)))

    def spot(self, axis, slot):
        return 9 * self.odd[axis] if slot else 9 - 9 * self.odd[axis]

    def kept(self, values, **slots):
        for axis, slot in slots.items():
            if slot:
                values = jnp.where(self.inner["xyz".index(axis)], values, jnp.zeros_like(values))
        return values


def gather_inner(place, cat, rims, arrays, stride, first, main, y0, y1, z0, z1):
    for at, arr in enumerate(arrays):
        base = at * stride + first
        inside = slice(base, base + 8)
        cat[inside, 1:9, :, 128:256] = main[arr]
        for side, face in ((0, y0), (1, y1)):
            part = place.kept(face[arr * 256 : arr * 256 + 256, :], y=side)
            cat[inside, place.spot(Y, side), :, 128:256] = part.reshape(8, 32, 128)
        for slot, own in ((0, z0), (1, z1)):
            rims[slot, inside, 1:9, :] = place.kept(own[arr].astype(F32), z=slot)
            for side, face in ((0, y0), (1, y1)):
                row = FACE + slot * 16 + arr * 8
                part = place.kept(face[row : row + 8, :].astype(F32), z=slot, y=side)
                for x in range(8):
                    rims[slot, base + x, pl.ds(place.spot(Y, side), 1), :] = part[x : x + 1, :]


def gather_outer(place, cat, rims, arrays, where, x0, x1):
    for at, arr in enumerate(arrays):
        for end, face in ((0, x0), (1, x1)):
            x = where(at, end)
            part = place.kept(face[arr * 256 : arr * 256 + 256, :], x=end)
            cat[x, 1:9, :, 128:256] = part.reshape(8, 32, 128)
            for side in range(2):
                row = FACE + side * 64 + arr * 32
                part = place.kept(face[row : row + 32, :], x=end, y=side)
                cat[x, place.spot(Y, side), :, 128:256] = part
            for slot in range(2):
                row = FACE + 128 + slot * 32 + arr * 16
                part = place.kept(face[row : row + 16, :].astype(F32), x=end, z=slot)
                rims[slot, x, 1:9, :] = part[1:9, :]
                rims[slot, x, pl.ds(place.spot(Y, 0), 1), :] = part[0:1, :]
                rims[slot, x, pl.ds(place.spot(Y, 1), 1), :] = place.kept(part[9:10, :], y=1)


def shift_slabs(place, cat, rims, count, where):
    spot = lax.broadcasted_iota(jnp.int32, (32, 128), 0)
    before, after = 1 - place.odd[Z], place.odd[Z]

    def step(i, _):
        x = where(i)
        for y in range(10):
            block = cat[x, y, :, 128:256].astype(F32)
            below = jnp.where(spot == 0, rims[before, x, y : y + 1, :], pltpu.roll(block, 1, 0))
            above = jnp.where(spot == 31, rims[after, x, y : y + 1, :], pltpu.roll(block, 31, 0))
            cat[x, y, :, 0:128] = below.astype(BF)
            cat[x, y, :, 256:384] = above.astype(BF)
        return 0

    lax.fori_loop(0, count, step, 0)


def convolve(slabs, weight):
    total = jnp.zeros((256, 256), F32)
    for half in range(2):
        for b in range(3):
            parts = [slab[b : b + 8].reshape(256, 384) for slab in slabs[half * 2 : half * 2 + 2]]
            total = total + jnp.dot(
                jnp.concatenate(parts, axis=1), weight[half * 3 + b], preferred_element_type=F32
            )
    return total[:, 0:128], total[:, 128:256]


def first_step(x, out_x, pairs, weights, occ, fields, turned, faces, slope, rows):
    for side, total in enumerate(convolve(pairs[0], weights[0])):
        mask = occ[x + side].reshape(256, 128).astype(F32)
        value = total * mask
        gate = jax.nn.sigmoid(value)
        hidden = value * gate
        slope[side] = gate * (1.0 + value * (1.0 - gate)) * mask
        keep_field(0, out_x + side, hidden, fields, turned, faces, rows)
    for side, total in enumerate(convolve(pairs[1], weights[1])):
        keep_field(1, out_x + side, total * slope[side], fields, turned, faces, rows)


def keep_field(arr, x, value, fields, turned, faces, rows):
    fields[arr, x] = value.astype(BF).reshape(8, 32, 128)
    columns = x * 256 if isinstance(x, int) else pl.multiple_of(x * 256, 256)
    turned[arr, :, pl.ds(columns, 256)] = value.T.astype(BF)
    z_faces(arr, x, value, rows, *faces)


def inner_kernel(main, y0, y1, z0, z1, occ, p1, t2, cat, fields, turned, q0, q1, rims, slope, rows):
    place = Places()
    gather_inner(place, cat, rims, (0, 1), 8, 0, main, y0, y1, z0, z1)
    shift_slabs(place, cat, rims, 16, lambda i: i)

    def step(i, _):
        x = 2 + 2 * i
        pairs = [[cat.at[arr * 8 + x - 1 + k] for k in range(4)] for arr in range(2)]
        first_step(x, 2 * i, pairs, (p1, t2), occ, fields, turned, (q0, q1), slope, rows)
        return 0

    lax.fori_loop(0, 2, step, 0)


def outer_kernel(x0, x1, cat, part, part_turned, f0, f1, occ, p1, t2, ends, fields, turned, q0, q1, rims, slope, rows):
    place = Places()
    gather_outer(place, ends, rims, (0, 1), lambda at, end: at * 2 + spot_end(place, end), x0, x1)
    shift_slabs(place, ends, rims, 4, lambda i: i)
    fields[:, 2:6] = part[...]
    turned[:, :, 512:1536] = part_turned[...]
    for q, f in ((q0, f0), (q1, f1)):
        q[:, 2:6] = f[...]
    low = [[ends.at[arr * 2]] + [cat.at[arr * 8 + k] for k in range(3)] for arr in range(2)]
    high = [[cat.at[arr * 8 + 5 + k] for k in range(3)] + [ends.at[arr * 2 + 1]] for arr in range(2)]
    for x, pairs in ((0, low), (6, high)):
        first_step(x, x, pairs, (p1, t2), occ, fields, turned, (q0, q1), slope, rows)


def spot_end(place, slot):
    return place.odd[X] if slot else 1 - place.odd[X]


def grads_kernel(arr, cat, ends, turned, wide, thin):
    left = turned[1 - arr]

    def slab(a, x, b):
        at = x + a
        ref = ends.at[arr * 2 + at // 9] if at in (0, 9) else cat.at[arr * 8 + at - 1]
        return ref[b : b + 8].reshape(256, 384)

    taps = [(a, b) for a in range(3) for b in range(3)]
    for start in range(0, 9, 2):
        group = taps[start : start + 2]
        right = [jnp.concatenate([slab(a, x, b) for x in range(8)], axis=0) for a, b in group]
        right = jnp.concatenate(right, axis=1) if len(right) > 1 else right[0]
        value = jnp.dot(left, right, preferred_element_type=F32)
        columns = slice(start * 384, start * 384 + 384 * len(group))
        if arr:
            pieces = [value[h * 64 + y * 16 : h * 64 + y * 16 + 16] for y in range(4) for h in range(2)]
            value = jnp.concatenate(pieces, axis=0)
        value = value.reshape(4, 32, -1)
        wide[:, :, columns] = value
        thin[:, :, columns] = value.astype(BF)


def heavy_call(kernel, out_shape, operands, scratch, limit, flops):
    total = sum(v.size * v.dtype.itemsize for v in operands)
    single = not isinstance(out_shape, tuple)
    return pl.pallas_call(
        kernel,
        out_shape=out_shape,
        in_specs=[VMEM] * len(operands),
        out_specs=VMEM if single else (VMEM,) * len(out_shape),
        scratch_shapes=scratch,
        compiler_params=pltpu.CompilerParams(vmem_limit_bytes=limit * MIB),
        cost_estimate=pl.CostEstimate(flops=flops, bytes_accessed=total, transcendentals=0),
    )(*operands)


def first_pass(main, halos, occ, p1, t2):
    x0, x1, y0, y1, z0, z1 = halos

    def outs(count):
        face = shape_of((2, count, 8, 128), BF)
        return (shape_of((2, count, 8, 32, 128), BF), shape_of((2, 128, count * 256), BF), face, face)

    def scratch(slabs):
        return [
            pltpu.VMEM((2, slabs, 16, 128), F32),
            pltpu.VMEM((2, 256, 128), F32),
            pltpu.VMEM((256, 128), F32),
        ]

    cat, part, part_turned, f0, f1 = heavy_call(
        inner_kernel,
        (shape_of((16, 10, 32, 384), BF),) + outs(4),
        (main, y0, y1, z0, z1, occ, p1, t2),
        scratch(16), 6, 2_000_000_000,
    )
    ends, fields, turned, q0, q1 = heavy_call(
        outer_kernel,
        (shape_of((4, 10, 32, 384), BF),) + outs(8),
        (x0, x1, cat, part, part_turned, f0, f1, occ, p1, t2),
        scratch(4), 4, 2_000_000_000,
    )
    grad = (shape_of((4, 32, 27 * 128), F32), shape_of((4, 32, 27 * 128), BF))
    second, first = (
        heavy_call(functools.partial(grads_kernel, arr), grad, (cat, ends, turned), [], 4, 2_000_000_000)
        for arr in (1, 0)
    )
    return fields, (q0, q1), first, second


def second_kernel(arr, main, x0, x1, y0, y1, z0, z1, occ, weight, out, cat, rims):
    place = Places()
    gather_inner(place, cat, rims, (arr,), 10, 1, main, y0, y1, z0, z1)
    gather_outer(place, cat, rims, (arr,), lambda at, end: place.spot(X, end), x0, x1)
    shift_slabs(place, cat, rims, 10, lambda i: i)

    def step(i, _):
        slabs = [cat.at[2 * i + k] for k in range(4)]
        for side, total in enumerate(convolve(slabs, weight)):
            mask = occ[2 * i + side].reshape(256, 128).astype(F32)
            out[2 * i + side] = (total * mask).astype(BF).reshape(8, 32, 128)
        return 0

    lax.fori_loop(0, 4, step, 0)


def second_pass(arr, main, halos, occ, weight):
    return heavy_call(
        functools.partial(second_kernel, arr),
        shape_of((8, 8, 32, 128), BF),
        (main, *halos, occ, weight),
        [pltpu.VMEM((10, 10, 32, 384), BF), pltpu.VMEM((2, 10, 16, 128), F32)],
        8, 2_000_000_000,
    )


def swap_faces(values, axis, slot):
    pairs = []
    for number in range(128):
        at = [number // 16, number // 4 % 4, number % 4]
        count, i = (8, 4, 4)[axis], at[axis]
        if slot == 0:
            at[axis] = i ^ 1
        elif axis == Z or 0 < i < count - 1:
            at[axis] = (i - 1 + 2 * (i % 2)) % count
        else:
            at[Z] ^= 1
        pairs.append((number, at[0] * 16 + at[1] * 4 + at[2]))
    return lax.ppermute(values, AXES, pairs)


def small_call(kernel, out_shape, operands, scratch=(), limit=2, inputs=None):
    single = not isinstance(out_shape, tuple)
    total = sum(v.size * v.dtype.itemsize for v in operands)
    return pl.pallas_call(
        kernel,
        out_shape=out_shape,
        in_specs=inputs or [VMEM] * len(operands),
        out_specs=VMEM if single else (VMEM,) * len(out_shape),
        scratch_shapes=scratch,
        compiler_params=pltpu.CompilerParams(vmem_limit_bytes=limit * MIB),
        cost_estimate=pl.CostEstimate(flops=0, bytes_accessed=total, transcendentals=0),
    )(*operands)


def z_faces(arr, x, values, rows, m0, m1):
    odd = place_on(Z)[1]
    rows[...] = values
    m0[arr, x] = rows[pl.ds(31 - 31 * odd, 8, stride=32), :].astype(BF)
    m1[arr, x] = rows[pl.ds(31 * odd, 8, stride=32), :].astype(BF)


def mask_kernel(bricks_far, features, cotangent, mask_far, main, occ, m0, m1, held, rows, mask, bricks, arrived, ready):
    flags_in = pltpu.make_async_copy(mask_far, mask, ready.at[0])
    bricks_in = pltpu.make_async_copy(bricks_far, bricks, ready.at[1])
    flags_in.start()
    bricks_in.start()
    copies = [
        [
            pltpu.make_async_copy(
                source.at[pl.ds(half * 4, 4)], held.at[arr, pl.ds(half * 4, 4)], arrived.at[arr, half]
            )
            for arr, source in ((0, features), (1, cotangent))
        ]
        for half in range(2)
    ]
    for pair in copies:
        for copy in pair:
            copy.start()
    flags_in.wait()
    bricks_in.wait()
    lane = lax.broadcasted_iota(jnp.int32, (8, 32), 1)
    active = jnp.zeros((8, 32), jnp.int32)
    for k in range(4):
        active = jnp.where(lane // BRICK == k, bricks[0, 0, k], active)
    diagonal = lax.broadcasted_iota(jnp.int32, (32, 32), 0) == lax.broadcasted_iota(jnp.int32, (32, 32), 1)
    ones = jnp.ones((32, 128), BF)
    for x in range(8):
        flags = (mask[x] * active).astype(F32)
        spread = [
            jnp.where(diagonal, jnp.broadcast_to(flags[y : y + 1], (32, 32)), 0.0) for y in range(8)
        ]
        wide = jnp.dot(jnp.concatenate(spread).astype(BF), ones, preferred_element_type=F32)
        occ[x] = wide.astype(BF).reshape(8, 32, 128)
    for x in range(8):
        if x % 4 == 0:
            for copy in copies[x // 4]:
                copy.wait()
        wide = occ[x].reshape(256, 128).astype(F32)
        for arr in range(2):
            masked = held[arr, x].reshape(256, 128).astype(F32) * wide
            main[arr, x] = masked.astype(BF).reshape(8, 32, 128)
            z_faces(arr, x, masked, rows, m0, m1)


def mask_inputs(features, cotangent, voxel_mask, brick_active):
    z_message = shape_of((2, 8, 8, 128), BF)
    far = pl.BlockSpec(memory_space=pltpu.HBM)
    return small_call(
        mask_kernel,
        (shape_of((2, 8, 8, 32, 128), BF), shape_of((8, 8, 32, 128), BF), z_message, z_message),
        [
            pltpu.with_memory_space_constraint(v, pltpu.HBM)
            for v in (brick_active, features, cotangent, voxel_mask)
        ],
        scratch=[
            pltpu.VMEM((2, 8, 8, 32, 128), BF),
            pltpu.VMEM((256, 128), F32),
            pltpu.VMEM((8, 8, 32), jnp.int32),
            pltpu.SMEM((1, 1, 4), jnp.int32),
            pltpu.SemaphoreType.DMA((2, 2)),
            pltpu.SemaphoreType.DMA((2,)),
        ],
        limit=4,
        inputs=[far] * 4,
    )


def y_kernel(main, z0, z1, m0, m1, own):
    odd = place_on(Y)[1]
    for slot, rims in ((0, z0), (1, z1)):
        own[slot] = rims[...].astype(F32).reshape(128, 128)
    for out, y in ((m0, 7 - 7 * odd), (m1, 7 * odd)):
        for arr in range(2):
            out[arr * 256 : arr * 256 + 256, :] = main[arr, :, y].reshape(256, 128)
            for slot in range(2):
                row = FACE + slot * 16 + arr * 8
                out[row : row + 8, :] = own[slot, pl.ds(arr * 64 + y, 8, stride=8), :].astype(BF)


def x_kernel(main, y0, y1, z0, z1, m0, m1, ends, piece):
    odd = place_on(X)[1]
    piece[...] = jnp.zeros_like(piece)
    for side, face in ((0, y0), (1, y1)):
        ends[side] = face[FACE : FACE + 32, :].astype(F32)
    for out, x in ((m0, 7 - 7 * odd), (m1, 7 * odd)):
        for arr in range(2):
            out[arr * 256 : arr * 256 + 256, :] = main[arr, x].reshape(256, 128)
            for side, face in ((0, y0), (1, y1)):
                row = FACE + side * 64 + arr * 32
                from_row = pl.multiple_of(arr * 256 + x * 32, 32)
                out[row : row + 32, :] = face[pl.ds(from_row, 32), :]
            for slot, rims in ((0, z0), (1, z1)):
                at = slot * 16 + arr * 8
                piece[0:1, :] = ends[0, pl.ds(at + x, 1), :]
                piece[1:9, :] = rims[arr, x].astype(F32)
                piece[9:10, :] = ends[1, pl.ds(at + x, 1), :]
                row = FACE + 128 + slot * 32 + arr * 16
                out[row : row + 16, :] = piece[...].astype(BF)


def exchange(main, messages):
    z0 = swap_faces(messages[0], Z, 0)
    z1 = swap_faces(messages[1], Z, 1)
    messages = small_call(
        y_kernel, (shape_of((544, 128), BF),) * 2, (main, z0, z1), scratch=[pltpu.VMEM((2, 128, 128), F32)]
    )
    y0 = swap_faces(messages[0], Y, 0)
    y1 = swap_faces(messages[1], Y, 1)
    messages = small_call(
        x_kernel,
        (shape_of((704, 128), BF),) * 2,
        (main, y0, y1, z0, z1),
        scratch=[pltpu.VMEM((2, 32, 128), F32), pltpu.VMEM((16, 128), F32)],
    )
    x0 = swap_faces(messages[0], X, 0)
    x1 = swap_faces(messages[1], X, 1)
    return x0, x1, y0, y1, z0, z1


def device_places():
    places = []
    for number in range(128):
        gx, gy, gz = number // 16, number // 4 % 4, number % 4
        places.append(((gx // 4) * 2 + gz // 2, gx % 4, gy, gz % 2))
    return places


def permute_chips(values, move):
    places = device_places()
    index = {place: number for number, place in enumerate(places)}
    pairs = [(n, index[move(*place)]) for n, place in enumerate(places)]
    return lax.ppermute(values, AXES, pairs)


def swap_cores(values):
    return permute_chips(values, lambda x, y, z, c: (x, y, z, 1 - c))


PARTNERS = (2, 1, 3)


def along_rows(flip):
    return lambda x, y, z, c: (x, y ^ (flip * c), z ^ (flip * (1 - c)), c)


def along_lanes(flip):
    return lambda x, y, z, c: (x, y ^ (flip * (1 - c)), z ^ (flip * c), c)


def along_x(flip):
    return lambda x, y, z, c: (x ^ flip, y, z, c)


def split_kernel(first, got_first, second, got_second, own, m1, m2, m3):
    _, y, z, core = chip_place()
    for which, block, keep, got in ((0, z, first, got_first), (1, y, second, got_second)):

        @pl.when(core == which)
        def _():
            for flip, out in zip((0,) + PARTNERS, (own, m1, m2, m3)):
                at = block ^ flip
                out[...] = (keep[at] + got[at].astype(F32)).astype(out.dtype)


def total_of(own, parts):
    r1, r2, r3 = (part[...].astype(F32) for part in parts)
    return own[...] + (r1 + r2) + r3


def halves_kernel(own, r1, r2, r3, kept, m1, m2, m3, whole):
    x, _, _, core = chip_place()
    whole[...] = total_of(own, (r1, r2, r3))
    for flip, out in zip((0,) + PARTNERS, (kept, m1, m2, m3)):
        chip = x ^ flip
        half = jnp.where(core == 0, chip & 1, chip >> 1)
        out[...] = whole[pl.ds(pl.multiple_of(half * 16, 16), 16), :].astype(out.dtype)


def sum_kernel(own, r1, r2, r3, total, message):
    value = total_of(own, (r1, r2, r3))
    total[...] = value
    message[...] = value.astype(BF)


def piece_kernel(factor, own, r1, r2, r3, piece):
    x, y, z, core = chip_place()
    block = jnp.where(core == 0, (x >> 1) * 4 + y, z * 2 + (x & 1))
    value = total_of(own, (r1, r2, r3)) * factor
    shift = (128 - block * 16) & 127
    for tap in range(27):
        at = jnp.where(core == 0, tap, 26 - tap)
        piece[at] = pltpu.roll(value[:, tap * 128 : tap * 128 + 128], shift, 1)
    for tap in range(27, 32):
        piece[tap] = jnp.zeros((16, 128), F32)


def outputs_kernel(mine, other, first, second, both):
    core = chip_place()[3]
    both[core] = mine[...].reshape(512, 128)
    both[1 - core] = other[...].reshape(512, 128)
    for j in range(8):
        turned = both[0, pl.ds(core * 8 + j, 32, stride=16), :].T
        first[pl.ds(j, 16, stride=8), :] = turned[0:16, 0:27]
    for i in range(16):
        turned = both[1, pl.ds(i, 32, stride=16), :].T
        second[i * 8 : i * 8 + 8, :] = jnp.where(core == 0, turned[0:8, 0:27], turned[8:16, 0:27])


def reduce_grads(first, second, factor):
    lanes = 27 * 128
    wide, thin = shape_of((32, lanes), BF), shape_of((16, lanes), BF)
    got_second = swap_cores(second[1])
    got_first = swap_cores(first[1])
    own, *messages = small_call(
        split_kernel, (shape_of((32, lanes), F32), wide, wide, wide), (first[0], got_first, second[0], got_second)
    )
    parts = [permute_chips(m, along_rows(PARTNERS[i])) for i, m in enumerate(messages)]
    own, *messages = small_call(
        halves_kernel,
        (shape_of((16, lanes), F32), thin, thin, thin),
        (own, *parts),
        scratch=[pltpu.VMEM((32, lanes), F32)],
    )
    parts = [permute_chips(m, along_x(PARTNERS[i])) for i, m in enumerate(messages)]
    own, message = small_call(sum_kernel, (shape_of((16, lanes), F32), thin), (own, *parts))
    parts = [permute_chips(message, along_lanes(PARTNERS[i])) for i in range(3)]
    piece = small_call(functools.partial(piece_kernel, factor), shape_of((32, 16, 128), F32), (own, *parts))
    other = swap_cores(piece)
    first, second = small_call(
        outputs_kernel, (shape_of((128, 27), F32),) * 2, (piece, other), scratch=[pltpu.VMEM((2, 512, 128), F32)]
    )
    return tuple(jnp.transpose(g.reshape(16, 8, 27), (2, 0, 1)) for g in (first, second))


def on_device(features, cotangent, voxel_mask, brick_active, first_weight, second_weight):
    factor = 1.0 / math.sqrt(voxel_mask.size * 128)
    main, occ, *faces = mask_inputs(features, cotangent, voxel_mask, brick_active)
    p1, t2 = prepare_weights(first_weight, second_weight)
    p2, t1 = prepare_weights(second_weight, first_weight)
    fields, next_faces, first, second = first_pass(main, exchange(main, faces), occ, p1, t2)
    halos = exchange(fields, next_faces)
    grad_first, grad_second = reduce_grads(first, second, factor)
    output_field = second_pass(0, fields, halos, occ, p2)
    grad_features = second_pass(1, fields, halos, occ, t1)
    return (output_field, grad_features, grad_first, grad_second)


def solution(mesh):
    return jax.shard_map(
        on_device,
        mesh=mesh,
        in_specs=(
            P("gx", "gy", "gz", None),
            P("gx", "gy", "gz", None),
            P("gx", "gy", "gz"),
            P("gx", "gy", "gz"),
            P(),
            P(),
        ),
        out_specs=(
            P("gx", "gy", "gz", None),
            P("gx", "gy", "gz", None),
            P(None, "gx", ("gy", "gz")),
            P(None, "gx", ("gy", "gz")),
        ),
        check_vma=False,
    )
```

```python
import functools
import math

import jax
import jax.numpy as jnp
from jax import lax
from jax.experimental import pallas as pl
from jax.experimental.pallas import tpu as pltpu
from jax.sharding import PartitionSpec as P


BRICK = 8
AXES = ("gx", "gy", "gz")
BF = jnp.bfloat16
F32 = jnp.float32
VMEM = pl.BlockSpec(memory_space=pltpu.VMEM)
SMEM = pl.BlockSpec(memory_space=pltpu.SMEM)
X, Y, Z = 0, 1, 2
FACE = 512
MIB = 1024 * 1024


def shape_of(shape, dtype):
    return jax.ShapeDtypeStruct(shape, dtype)


def weights_kernel(wp, wt, pairs, flipped):
    zero = jnp.zeros((128, 128), BF)

    def forward(t):
        return wp[t]

    def backward(t):
        return wt[26 - t].astype(F32).T.astype(BF)

    for out, get in ((pairs, forward), (flipped, backward)):
        for b in range(3):
            for c in range(3):
                taps = [get(a * 9 + b * 3 + c) for a in range(3)]
                for s in range(4):
                    group, k = (s // 2) * 3 + b, (s % 2) * 384 + c * 128
                    out[group, k : k + 128, 0:128] = taps[s] if s < 3 else zero
                    out[group, k : k + 128, 128:256] = taps[s - 1] if s > 0 else zero


def prepare_weights(paired, turned):
    one = shape_of((6, 768, 256), BF)
    return pl.pallas_call(
        weights_kernel,
        out_shape=(one,) * 2,
        in_specs=[VMEM] * 2,
        out_specs=(VMEM,) * 2,
        compiler_params=pltpu.CompilerParams(vmem_limit_bytes=12 * MIB),
        cost_estimate=pl.CostEstimate(flops=0, bytes_accessed=6_500_000, transcendentals=0),
        name="weights",
    )(paired, turned)


def place_on(axis):
    at = lax.axis_index(AXES[axis])
    return at, at & 1, (at != 0) & (at != lax.axis_size(AXES[axis]) - 1)


def chip_place():
    gx, gy, gz = (lax.axis_index(name) for name in AXES)
    return (gx >> 2) * 2 + (gz >> 1), gx & 3, gy, gz & 1


class Places:
    def __init__(self):
        self.odd, self.inner = zip(*(place_on(axis)[1:] for axis in range(3)))

    def spot(self, axis, slot):
        return 9 * self.odd[axis] if slot else 9 - 9 * self.odd[axis]

    def kept(self, values, **slots):
        for axis, slot in slots.items():
            if slot:
                values = jnp.where(self.inner["xyz".index(axis)], values, jnp.zeros_like(values))
        return values


def gather_inner(place, cat, rims, arrays, stride, first, main, y0, y1, e0, e1, edge, z0, z1):
    for at, arr in enumerate(arrays):
        base = at * stride + first
        inside = slice(base, base + 8)
        cat[inside, 1:9, :, 128:256] = main[arr]
        for side, face in ((0, y0), (1, y1)):
            part = place.kept(face[arr * 256 : arr * 256 + 256, :], y=side)
            cat[inside, place.spot(Y, side), :, 128:256] = part.reshape(8, 32, 128)
        for slot, own in ((0, z0), (1, z1)):
            rims[slot, inside, 1:9, :] = place.kept(own[arr].astype(F32), z=slot)
            for side, face in ((0, e0), (1, e1)):
                row = edge + slot * 16 + arr * 8
                part = place.kept(face[row : row + 8, :].astype(F32), z=slot, y=side)
                for x in range(8):
                    rims[slot, base + x, pl.ds(place.spot(Y, side), 1), :] = part[x : x + 1, :]


def gather_outer(place, cat, rims, arrays, where, x0, x1):
    for at, arr in enumerate(arrays):
        for end, face in ((0, x0), (1, x1)):
            x = where(at, end)
            part = place.kept(face[arr * 256 : arr * 256 + 256, :], x=end)
            cat[x, 1:9, :, 128:256] = part.reshape(8, 32, 128)
            for side in range(2):
                row = FACE + side * 64 + arr * 32
                part = place.kept(face[row : row + 32, :], x=end, y=side)
                cat[x, place.spot(Y, side), :, 128:256] = part
            for slot in range(2):
                row = FACE + 128 + slot * 32 + arr * 16
                part = place.kept(face[row : row + 16, :].astype(F32), x=end, z=slot)
                rims[slot, x, 1:9, :] = part[1:9, :]
                rims[slot, x, pl.ds(place.spot(Y, 0), 1), :] = part[0:1, :]
                rims[slot, x, pl.ds(place.spot(Y, 1), 1), :] = place.kept(part[9:10, :], y=1)


def shift_slabs(place, cat, rims, count, where):
    spot = lax.broadcasted_iota(jnp.int32, (32, 128), 0)
    before, after = 1 - place.odd[Z], place.odd[Z]

    def step(i, _):
        x = where(i)
        for y in range(10):
            block = cat[x, y, :, 128:256].astype(F32)
            below = jnp.where(spot == 0, rims[before, x, y : y + 1, :], pltpu.roll(block, 1, 0))
            above = jnp.where(spot == 31, rims[after, x, y : y + 1, :], pltpu.roll(block, 31, 0))
            cat[x, y, :, 0:128] = below.astype(BF)
            cat[x, y, :, 256:384] = above.astype(BF)
        return 0

    lax.fori_loop(0, count, step, 0)


def convolve(slabs, weight):
    total = jnp.zeros((256, 256), F32)
    for half in range(2):
        for b in range(3):
            parts = [slab[b : b + 8].reshape(256, 384) for slab in slabs[half * 2 : half * 2 + 2]]
            total = total + jnp.dot(
                jnp.concatenate(parts, axis=1), weight[half * 3 + b], preferred_element_type=F32
            )
    return total[:, 0:128], total[:, 128:256]


def first_step(x, out_x, pairs, weights, occ, fields, turned, faces, slope, rows):
    for side, total in enumerate(convolve(pairs[0], weights[0])):
        mask = occ[x + side].reshape(256, 128).astype(F32)
        value = total * mask
        gate = jax.nn.sigmoid(value)
        hidden = value * gate
        slope[side] = gate * (1.0 + value * (1.0 - gate)) * mask
        keep_field(0, out_x + side, hidden, fields, turned, faces, rows)
    for side, total in enumerate(convolve(pairs[1], weights[1])):
        keep_field(1, out_x + side, total * slope[side], fields, turned, faces, rows)


def keep_field(arr, x, value, fields, turned, faces, rows):
    fields[arr, x] = value.astype(BF).reshape(8, 32, 128)
    columns = x * 256 if isinstance(x, int) else pl.multiple_of(x * 256, 256)
    turned[arr, :, pl.ds(columns, 256)] = value.T.astype(BF)
    z_faces(arr, x, value, rows, *faces)


def inner_kernel(main, y0, y1, e0, e1, z0, z1, occ, p1, t2, cat, fields, turned, q0, q1, rims, slope, rows):
    place = Places()
    gather_inner(place, cat, rims, (0, 1), 8, 0, main, y0, y1, e0, e1, 0, z0, z1)
    shift_slabs(place, cat, rims, 16, lambda i: i)

    def step(i, _):
        x = 2 + 2 * i
        pairs = [[cat.at[arr * 8 + x - 1 + k] for k in range(4)] for arr in range(2)]
        first_step(x, 2 * i, pairs, (p1, t2), occ, fields, turned, (q0, q1), slope, rows)
        return 0

    lax.fori_loop(0, 2, step, 0)


def outer_kernel(x0, x1, cat, part, part_turned, f0, f1, occ, p1, t2, ends, fields, turned, q0, q1, rims, slope, rows):
    place = Places()
    gather_outer(place, ends, rims, (0, 1), lambda at, end: at * 2 + spot_end(place, end), x0, x1)
    shift_slabs(place, ends, rims, 4, lambda i: i)
    fields[:, 2:6] = part[...]
    turned[:, :, 512:1536] = part_turned[...]
    for q, f in ((q0, f0), (q1, f1)):
        q[:, 2:6] = f[...]
    low = [[ends.at[arr * 2]] + [cat.at[arr * 8 + k] for k in range(3)] for arr in range(2)]
    high = [[cat.at[arr * 8 + 5 + k] for k in range(3)] + [ends.at[arr * 2 + 1]] for arr in range(2)]
    for x, pairs in ((0, low), (6, high)):
        first_step(x, x, pairs, (p1, t2), occ, fields, turned, (q0, q1), slope, rows)


def spot_end(place, slot):
    return place.odd[X] if slot else 1 - place.odd[X]


def grads_kernel(arr, cat, ends, turned, wide, thin):
    left = turned[1 - arr]

    def slab(a, x, b):
        at = x + a
        ref = ends.at[arr * 2 + at // 9] if at in (0, 9) else cat.at[arr * 8 + at - 1]
        return ref[b : b + 8].reshape(256, 384)

    taps = [(a, b) for a in range(3) for b in range(3)]
    for start in range(0, 9, 2):
        group = taps[start : start + 2]
        right = [jnp.concatenate([slab(a, x, b) for x in range(8)], axis=0) for a, b in group]
        right = jnp.concatenate(right, axis=1) if len(right) > 1 else right[0]
        value = jnp.dot(left, right, preferred_element_type=F32)
        columns = slice(start * 384, start * 384 + 384 * len(group))
        if arr:
            pieces = [value[h * 64 + y * 16 : h * 64 + y * 16 + 16] for y in range(4) for h in range(2)]
            value = jnp.concatenate(pieces, axis=0)
        value = value.reshape(4, 32, -1)
        wide[:, :, columns] = value
        thin[:, :, columns] = value.astype(BF)


def heavy_call(kernel, out_shape, operands, scratch, limit, flops):
    total = sum(v.size * v.dtype.itemsize for v in operands)
    single = not isinstance(out_shape, tuple)
    return pl.pallas_call(
        kernel,
        out_shape=out_shape,
        in_specs=[VMEM] * len(operands),
        out_specs=VMEM if single else (VMEM,) * len(out_shape),
        scratch_shapes=scratch,
        compiler_params=pltpu.CompilerParams(vmem_limit_bytes=limit * MIB),
        cost_estimate=pl.CostEstimate(flops=flops, bytes_accessed=total, transcendentals=0),
    )(*operands)


def first_pass(main, halos, occ, p1, t2):
    x0, x1, y0, y1, e0, e1, z0, z1 = halos

    def outs(count):
        face = shape_of((2, count, 8, 128), BF)
        return (shape_of((2, count, 8, 32, 128), BF), shape_of((2, 128, count * 256), BF), face, face)

    def scratch(slabs):
        return [
            pltpu.VMEM((2, slabs, 16, 128), F32),
            pltpu.VMEM((2, 256, 128), F32),
            pltpu.VMEM((256, 128), F32),
        ]

    cat, part, part_turned, f0, f1 = heavy_call(
        inner_kernel,
        (shape_of((16, 10, 32, 384), BF),) + outs(4),
        (main, y0, y1, e0, e1, z0, z1, occ, p1, t2),
        scratch(16), 6, 2_000_000_000,
    )
    ends, fields, turned, q0, q1 = heavy_call(
        outer_kernel,
        (shape_of((4, 10, 32, 384), BF),) + outs(8),
        (x0, x1, cat, part, part_turned, f0, f1, occ, p1, t2),
        scratch(4), 4, 2_000_000_000,
    )
    grad = (shape_of((4, 32, 27 * 128), F32), shape_of((4, 32, 27 * 128), BF))
    second, first = (
        heavy_call(functools.partial(grads_kernel, arr), grad, (cat, ends, turned), [], 4, 2_000_000_000)
        for arr in (1, 0)
    )
    return fields, (q0, q1), first, second


def second_kernel(arr, main, x0, x1, y0, y1, z0, z1, occ, weight, out, cat, rims):
    place = Places()
    gather_inner(place, cat, rims, (arr,), 10, 1, main, y0, y1, y0, y1, FACE, z0, z1)
    gather_outer(place, cat, rims, (arr,), lambda at, end: place.spot(X, end), x0, x1)
    shift_slabs(place, cat, rims, 10, lambda i: i)

    def step(i, _):
        slabs = [cat.at[2 * i + k] for k in range(4)]
        for side, total in enumerate(convolve(slabs, weight)):
            mask = occ[2 * i + side].reshape(256, 128).astype(F32)
            out[2 * i + side] = (total * mask).astype(BF).reshape(8, 32, 128)
        return 0

    lax.fori_loop(0, 4, step, 0)


def second_pass(arr, main, halos, occ, weight):
    return heavy_call(
        functools.partial(second_kernel, arr),
        shape_of((8, 8, 32, 128), BF),
        (main, *halos, occ, weight),
        [pltpu.VMEM((10, 10, 32, 384), BF), pltpu.VMEM((2, 10, 16, 128), F32)],
        8, 2_000_000_000,
    )


def swap_faces(values, axis, slot):
    pairs = []
    for number in range(128):
        at = [number // 16, number // 4 % 4, number % 4]
        count, i = (8, 4, 4)[axis], at[axis]
        if slot == 0:
            at[axis] = i ^ 1
        elif axis == Z or 0 < i < count - 1:
            at[axis] = (i - 1 + 2 * (i % 2)) % count
        else:
            at[Z] ^= 1
        pairs.append((number, at[0] * 16 + at[1] * 4 + at[2]))
    return lax.ppermute(values, AXES, pairs)


def small_call(kernel, out_shape, operands, scratch=(), limit=2, inputs=None):
    single = not isinstance(out_shape, tuple)
    total = sum(v.size * v.dtype.itemsize for v in operands)
    return pl.pallas_call(
        kernel,
        out_shape=out_shape,
        in_specs=inputs or [VMEM] * len(operands),
        out_specs=VMEM if single else (VMEM,) * len(out_shape),
        scratch_shapes=scratch,
        compiler_params=pltpu.CompilerParams(vmem_limit_bytes=limit * MIB),
        cost_estimate=pl.CostEstimate(flops=0, bytes_accessed=total, transcendentals=0),
    )(*operands)


def z_faces(arr, x, values, rows, m0, m1):
    odd = place_on(Z)[1]
    rows[...] = values
    m0[arr, x] = rows[pl.ds(31 - 31 * odd, 8, stride=32), :].astype(BF)
    m1[arr, x] = rows[pl.ds(31 * odd, 8, stride=32), :].astype(BF)


def mask_kernel(bricks_far, features, cotangent, mask_far, main, occ, m0, m1, f0, f1, held, rows, mask, bricks, arrived, ready):
    flags_in = pltpu.make_async_copy(mask_far, mask, ready.at[0])
    bricks_in = pltpu.make_async_copy(bricks_far, bricks, ready.at[1])
    flags_in.start()
    bricks_in.start()
    copies = [
        [
            pltpu.make_async_copy(
                source.at[pl.ds(half * 4, 4)], held.at[arr, pl.ds(half * 4, 4)], arrived.at[arr, half]
            )
            for arr, source in ((0, features), (1, cotangent))
        ]
        for half in range(2)
    ]
    for pair in copies:
        for copy in pair:
            copy.start()
    flags_in.wait()
    bricks_in.wait()
    lane = lax.broadcasted_iota(jnp.int32, (8, 32), 1)
    active = jnp.zeros((8, 32), jnp.int32)
    for k in range(4):
        active = jnp.where(lane // BRICK == k, bricks[0, 0, k], active)
    diagonal = lax.broadcasted_iota(jnp.int32, (32, 32), 0) == lax.broadcasted_iota(jnp.int32, (32, 32), 1)
    ones = jnp.ones((32, 128), BF)
    for x in range(8):
        flags = (mask[x] * active).astype(F32)
        spread = [
            jnp.where(diagonal, jnp.broadcast_to(flags[y : y + 1], (32, 32)), 0.0) for y in range(8)
        ]
        wide = jnp.dot(jnp.concatenate(spread).astype(BF), ones, preferred_element_type=F32)
        occ[x] = wide.astype(BF).reshape(8, 32, 128)
    odd = place_on(Y)[1]
    for x in range(8):
        if x % 4 == 0:
            for copy in copies[x // 4]:
                copy.wait()
        wide = occ[x].reshape(256, 128).astype(F32)
        for arr in range(2):
            masked = held[arr, x].reshape(256, 128).astype(F32) * wide
            main[arr, x] = masked.astype(BF).reshape(8, 32, 128)
            z_faces(arr, x, masked, rows, m0, m1)
            row = arr * 256 + x * 32
            f0[row : row + 32, :] = main[arr, x, 7 - 7 * odd]
            f1[row : row + 32, :] = main[arr, x, 7 * odd]


def mask_inputs(features, cotangent, voxel_mask, brick_active):
    z_message, y_message = shape_of((2, 8, 8, 128), BF), shape_of((FACE, 128), BF)
    far = pl.BlockSpec(memory_space=pltpu.HBM)
    return small_call(
        mask_kernel,
        (shape_of((2, 8, 8, 32, 128), BF), shape_of((8, 8, 32, 128), BF), z_message, z_message, y_message, y_message),
        [
            pltpu.with_memory_space_constraint(v, pltpu.HBM)
            for v in (brick_active, features, cotangent, voxel_mask)
        ],
        scratch=[
            pltpu.VMEM((2, 8, 8, 32, 128), BF),
            pltpu.VMEM((256, 128), F32),
            pltpu.VMEM((8, 8, 32), jnp.int32),
            pltpu.SMEM((1, 1, 4), jnp.int32),
            pltpu.SemaphoreType.DMA((2, 2)),
            pltpu.SemaphoreType.DMA((2,)),
        ],
        limit=4,
        inputs=[far] * 4,
    )


def y_kernel(main, z0, z1, m0, m1, own):
    odd = place_on(Y)[1]
    for slot, rims in ((0, z0), (1, z1)):
        own[slot] = rims[...].astype(F32).reshape(128, 128)
    for out, y in ((m0, 7 - 7 * odd), (m1, 7 * odd)):
        for arr in range(2):
            out[arr * 256 : arr * 256 + 256, :] = main[arr, :, y].reshape(256, 128)
            for slot in range(2):
                row = FACE + slot * 16 + arr * 8
                out[row : row + 8, :] = own[slot, pl.ds(arr * 64 + y, 8, stride=8), :].astype(BF)


def edge_kernel(z0, z1, m0, m1, own):
    odd = place_on(Y)[1]
    for slot, rims in ((0, z0), (1, z1)):
        own[slot] = rims[...].astype(F32).reshape(128, 128)
    for out, y in ((m0, 7 - 7 * odd), (m1, 7 * odd)):
        for arr in range(2):
            for slot in range(2):
                row = slot * 16 + arr * 8
                out[row : row + 8, :] = own[slot, pl.ds(arr * 64 + y, 8, stride=8), :].astype(BF)


def x_kernel(edge, main, y0, y1, e0, e1, z0, z1, m0, m1, ends, piece):
    odd = place_on(X)[1]
    piece[...] = jnp.zeros_like(piece)
    for side, face in ((0, e0), (1, e1)):
        ends[side] = face[edge : edge + 32, :].astype(F32)
    for out, x in ((m0, 7 - 7 * odd), (m1, 7 * odd)):
        for arr in range(2):
            out[arr * 256 : arr * 256 + 256, :] = main[arr, x].reshape(256, 128)
            for side, face in ((0, y0), (1, y1)):
                row = FACE + side * 64 + arr * 32
                from_row = pl.multiple_of(arr * 256 + x * 32, 32)
                out[row : row + 32, :] = face[pl.ds(from_row, 32), :]
            for slot, rims in ((0, z0), (1, z1)):
                at = slot * 16 + arr * 8
                piece[0:1, :] = ends[0, pl.ds(at + x, 1), :]
                piece[1:9, :] = rims[arr, x].astype(F32)
                piece[9:10, :] = ends[1, pl.ds(at + x, 1), :]
                row = FACE + 128 + slot * 32 + arr * 16
                out[row : row + 16, :] = piece[...].astype(BF)


def exchange_x(main, y0, y1, e0, e1, edge, z0, z1):
    messages = small_call(
        functools.partial(x_kernel, edge),
        (shape_of((704, 128), BF),) * 2,
        (main, y0, y1, e0, e1, z0, z1),
        scratch=[pltpu.VMEM((2, 32, 128), F32), pltpu.VMEM((16, 128), F32)],
    )
    x0 = swap_faces(messages[0], X, 0)
    x1 = swap_faces(messages[1], X, 1)
    return x0, x1


def exchange_first(main, messages, faces):
    z0 = swap_faces(messages[0], Z, 0)
    z1 = swap_faces(messages[1], Z, 1)
    y0 = swap_faces(faces[0], Y, 0)
    y1 = swap_faces(faces[1], Y, 1)
    edges = small_call(edge_kernel, (shape_of((32, 128), BF),) * 2, (z0, z1), scratch=[pltpu.VMEM((2, 128, 128), F32)])
    e0 = swap_faces(edges[0], Y, 0)
    e1 = swap_faces(edges[1], Y, 1)
    x0, x1 = exchange_x(main, y0, y1, e0, e1, 0, z0, z1)
    return x0, x1, y0, y1, e0, e1, z0, z1


def exchange_second(main, messages):
    z0 = swap_faces(messages[0], Z, 0)
    z1 = swap_faces(messages[1], Z, 1)
    messages = small_call(
        y_kernel, (shape_of((544, 128), BF),) * 2, (main, z0, z1), scratch=[pltpu.VMEM((2, 128, 128), F32)]
    )
    y0 = swap_faces(messages[0], Y, 0)
    y1 = swap_faces(messages[1], Y, 1)
    x0, x1 = exchange_x(main, y0, y1, y0, y1, FACE, z0, z1)
    return x0, x1, y0, y1, z0, z1


def device_places():
    places = []
    for number in range(128):
        gx, gy, gz = number // 16, number // 4 % 4, number % 4
        places.append(((gx // 4) * 2 + gz // 2, gx % 4, gy, gz % 2))
    return places


def permute_chips(values, move):
    places = device_places()
    index = {place: number for number, place in enumerate(places)}
    pairs = [(n, index[move(*place)]) for n, place in enumerate(places)]
    return lax.ppermute(values, AXES, pairs)


def swap_cores(values):
    return permute_chips(values, lambda x, y, z, c: (x, y, z, 1 - c))


PARTNERS = (2, 1, 3)


def along_rows(flip):
    return lambda x, y, z, c: (x, y ^ (flip * c), z ^ (flip * (1 - c)), c)


def along_lanes(flip):
    return lambda x, y, z, c: (x, y ^ (flip * (1 - c)), z ^ (flip * c), c)


def along_x(flip):
    return lambda x, y, z, c: (x ^ flip, y, z, c)


def split_kernel(first, got_first, second, got_second, own, m1, m2, m3):
    _, y, z, core = chip_place()
    for which, block, keep, got in ((0, z, first, got_first), (1, y, second, got_second)):

        @pl.when(core == which)
        def _():
            for flip, out in zip((0,) + PARTNERS, (own, m1, m2, m3)):
                at = block ^ flip
                out[...] = (keep[at] + got[at].astype(F32)).astype(out.dtype)


def total_of(own, parts):
    r1, r2, r3 = (part[...].astype(F32) for part in parts)
    return own[...] + (r1 + r2) + r3


def halves_kernel(own, r1, r2, r3, kept, m1, m2, m3, whole):
    x, _, _, core = chip_place()
    whole[...] = total_of(own, (r1, r2, r3))
    for flip, out in zip((0,) + PARTNERS, (kept, m1, m2, m3)):
        chip = x ^ flip
        half = jnp.where(core == 0, chip & 1, chip >> 1)
        out[...] = whole[pl.ds(pl.multiple_of(half * 16, 16), 16), :].astype(out.dtype)


def sum_kernel(own, r1, r2, r3, total, message):
    value = total_of(own, (r1, r2, r3))
    total[...] = value
    message[...] = value.astype(BF)


def piece_kernel(factor, own, r1, r2, r3, piece):
    x, y, z, core = chip_place()
    block = jnp.where(core == 0, (x >> 1) * 4 + y, z * 2 + (x & 1))
    value = total_of(own, (r1, r2, r3)) * factor
    shift = (128 - block * 16) & 127
    for tap in range(27):
        at = jnp.where(core == 0, tap, 26 - tap)
        piece[at] = pltpu.roll(value[:, tap * 128 : tap * 128 + 128], shift, 1)
    for tap in range(27, 32):
        piece[tap] = jnp.zeros((16, 128), F32)


def outputs_kernel(mine, other, first, second, both):
    core = chip_place()[3]
    both[core] = mine[...].reshape(512, 128)
    both[1 - core] = other[...].reshape(512, 128)
    for j in range(8):
        turned = both[0, pl.ds(core * 8 + j, 32, stride=16), :].T
        first[pl.ds(j, 16, stride=8), :] = turned[0:16, 0:27]
    for i in range(16):
        turned = both[1, pl.ds(i, 32, stride=16), :].T
        second[i * 8 : i * 8 + 8, :] = jnp.where(core == 0, turned[0:8, 0:27], turned[8:16, 0:27])


def reduce_grads(first, second, factor):
    lanes = 27 * 128
    wide, thin = shape_of((32, lanes), BF), shape_of((16, lanes), BF)
    got_second = swap_cores(second[1])
    got_first = swap_cores(first[1])
    own, *messages = small_call(
        split_kernel, (shape_of((32, lanes), F32), wide, wide, wide), (first[0], got_first, second[0], got_second)
    )
    parts = [permute_chips(m, along_rows(PARTNERS[i])) for i, m in enumerate(messages)]
    own, *messages = small_call(
        halves_kernel,
        (shape_of((16, lanes), F32), thin, thin, thin),
        (own, *parts),
        scratch=[pltpu.VMEM((32, lanes), F32)],
    )
    parts = [permute_chips(m, along_x(PARTNERS[i])) for i, m in enumerate(messages)]
    own, message = small_call(sum_kernel, (shape_of((16, lanes), F32), thin), (own, *parts))
    parts = [permute_chips(message, along_lanes(PARTNERS[i])) for i in range(3)]
    piece = small_call(functools.partial(piece_kernel, factor), shape_of((32, 16, 128), F32), (own, *parts))
    other = swap_cores(piece)
    first, second = small_call(
        outputs_kernel, (shape_of((128, 27), F32),) * 2, (piece, other), scratch=[pltpu.VMEM((2, 512, 128), F32)]
    )
    return tuple(jnp.transpose(g.reshape(16, 8, 27), (2, 0, 1)) for g in (first, second))


def on_device(features, cotangent, voxel_mask, brick_active, first_weight, second_weight):
    factor = 1.0 / math.sqrt(voxel_mask.size * 128)
    main, occ, m0, m1, f0, f1 = mask_inputs(features, cotangent, voxel_mask, brick_active)
    p1, t2 = prepare_weights(first_weight, second_weight)
    p2, t1 = prepare_weights(second_weight, first_weight)
    fields, next_faces, first, second = first_pass(main, exchange_first(main, (m0, m1), (f0, f1)), occ, p1, t2)
    halos = exchange_second(fields, next_faces)
    grad_first, grad_second = reduce_grads(first, second, factor)
    output_field = second_pass(0, fields, halos, occ, p2)
    grad_features = second_pass(1, fields, halos, occ, t1)
    return (output_field, grad_features, grad_first, grad_second)


def solution(mesh):
    return jax.shard_map(
        on_device,
        mesh=mesh,
        in_specs=(
            P("gx", "gy", "gz", None),
            P("gx", "gy", "gz", None),
            P("gx", "gy", "gz"),
            P("gx", "gy", "gz"),
            P(),
            P(),
        ),
        out_specs=(
            P("gx", "gy", "gz", None),
            P("gx", "gy", "gz", None),
            P(None, "gx", ("gy", "gz")),
            P(None, "gx", ("gy", "gz")),
        ),
        check_vma=False,
    )
```

```python
import functools
import math

import jax
import jax.numpy as jnp
from jax import lax
from jax.experimental import pallas as pl
from jax.experimental.pallas import tpu as pltpu
from jax.sharding import PartitionSpec as P


BRICK = 8
AXES = ("gx", "gy", "gz")
BF = jnp.bfloat16
F32 = jnp.float32
VMEM = pl.BlockSpec(memory_space=pltpu.VMEM)
SMEM = pl.BlockSpec(memory_space=pltpu.SMEM)
X, Y, Z = 0, 1, 2
FACE = 512
MIB = 1024 * 1024


def shape_of(shape, dtype):
    return jax.ShapeDtypeStruct(shape, dtype)


def weights_kernel(far_p, far_t, pairs, flipped, wp, wt, arrived):
    copies = [
        [
            pltpu.make_async_copy(far.at[pl.ds(9 * a, 9)], near.at[pl.ds(9 * a, 9)], arrived.at[i, a])
            for a in range(3)
        ]
        for i, (far, near) in enumerate(((far_p, wp), (far_t, wt)))
    ]
    for group in copies:
        for copy in group:
            copy.start()
    zero = jnp.zeros((128, 128), BF)

    def forward(t):
        return wp[t]

    def backward(t):
        return wt[26 - t].astype(F32).T.astype(BF)

    for group, out, get in ((copies[0], pairs, forward), (copies[1], flipped, backward)):
        for copy in group:
            copy.wait()
        for b in range(3):
            for c in range(3):
                taps = [get(a * 9 + b * 3 + c) for a in range(3)]
                for s in range(4):
                    group, k = (s // 2) * 3 + b, (s % 2) * 384 + c * 128
                    out[group, k : k + 128, 0:128] = taps[s] if s < 3 else zero
                    out[group, k : k + 128, 128:256] = taps[s - 1] if s > 0 else zero


def prepare_weights(paired, turned):
    one = shape_of((6, 768, 256), BF)
    near = pltpu.VMEM((27, 128, 128), BF)
    return pl.pallas_call(
        weights_kernel,
        out_shape=(one,) * 2,
        in_specs=[pl.BlockSpec(memory_space=pltpu.HBM)] * 2,
        out_specs=(VMEM,) * 2,
        scratch_shapes=[near, near, pltpu.SemaphoreType.DMA((2, 3))],
        compiler_params=pltpu.CompilerParams(vmem_limit_bytes=6 * MIB),
        cost_estimate=pl.CostEstimate(flops=0, bytes_accessed=6_500_000, transcendentals=0),
        name="weights",
    )(*(pltpu.with_memory_space_constraint(v, pltpu.HBM) for v in (paired, turned)))


def place_on(axis):
    at = lax.axis_index(AXES[axis])
    return at, at & 1, (at != 0) & (at != lax.axis_size(AXES[axis]) - 1)


def chip_place():
    gx, gy, gz = (lax.axis_index(name) for name in AXES)
    return (gx >> 2) * 2 + (gz >> 1), gx & 3, gy, gz & 1


class Places:
    def __init__(self):
        self.odd, self.inner = zip(*(place_on(axis)[1:] for axis in range(3)))

    def spot(self, axis, slot):
        return 9 * self.odd[axis] if slot else 9 - 9 * self.odd[axis]

    def kept(self, values, **slots):
        for axis, slot in slots.items():
            if slot:
                values = jnp.where(self.inner["xyz".index(axis)], values, jnp.zeros_like(values))
        return values


def gather_inner(place, cat, rims, arrays, stride, first, main, y0, y1, e0, e1, edge, z0, z1):
    for at, arr in enumerate(arrays):
        base = at * stride + first
        inside = slice(base, base + 8)
        cat[inside, 1:9, :, 128:256] = main[arr]
        for side, face in ((0, y0), (1, y1)):
            part = place.kept(face[arr * 256 : arr * 256 + 256, :], y=side)
            cat[inside, place.spot(Y, side), :, 128:256] = part.reshape(8, 32, 128)
        for slot, own in ((0, z0), (1, z1)):
            rims[slot, inside, 1:9, :] = place.kept(own[arr].astype(F32), z=slot)
            for side, face in ((0, e0), (1, e1)):
                row = edge + slot * 16 + arr * 8
                part = place.kept(face[row : row + 8, :].astype(F32), z=slot, y=side)
                for x in range(8):
                    rims[slot, base + x, pl.ds(place.spot(Y, side), 1), :] = part[x : x + 1, :]


def gather_outer(place, cat, rims, arrays, where, x0, x1):
    for at, arr in enumerate(arrays):
        for end, face in ((0, x0), (1, x1)):
            x = where(at, end)
            part = place.kept(face[arr * 256 : arr * 256 + 256, :], x=end)
            cat[x, 1:9, :, 128:256] = part.reshape(8, 32, 128)
            for side in range(2):
                row = FACE + side * 64 + arr * 32
                part = place.kept(face[row : row + 32, :], x=end, y=side)
                cat[x, place.spot(Y, side), :, 128:256] = part
            for slot in range(2):
                row = FACE + 128 + slot * 32 + arr * 16
                part = place.kept(face[row : row + 16, :].astype(F32), x=end, z=slot)
                rims[slot, x, 1:9, :] = part[1:9, :]
                rims[slot, x, pl.ds(place.spot(Y, 0), 1), :] = part[0:1, :]
                rims[slot, x, pl.ds(place.spot(Y, 1), 1), :] = place.kept(part[9:10, :], y=1)


def shift_slabs(place, cat, rims, count, where):
    spot = lax.broadcasted_iota(jnp.int32, (32, 128), 0)
    before, after = 1 - place.odd[Z], place.odd[Z]

    def step(i, _):
        x = where(i)
        for y in range(10):
            block = cat[x, y, :, 128:256].astype(F32)
            below = jnp.where(spot == 0, rims[before, x, y : y + 1, :], pltpu.roll(block, 1, 0))
            above = jnp.where(spot == 31, rims[after, x, y : y + 1, :], pltpu.roll(block, 31, 0))
            cat[x, y, :, 0:128] = below.astype(BF)
            cat[x, y, :, 256:384] = above.astype(BF)
        return 0

    lax.fori_loop(0, count, step, 0)


def convolve(slabs, weight):
    total = jnp.zeros((256, 256), F32)
    for half in range(2):
        for b in range(3):
            parts = [slab[b : b + 8].reshape(256, 384) for slab in slabs[half * 2 : half * 2 + 2]]
            total = total + jnp.dot(
                jnp.concatenate(parts, axis=1), weight[half * 3 + b], preferred_element_type=F32
            )
    return total[:, 0:128], total[:, 128:256]


def first_step(x, out_x, pairs, weights, occ, fields, turned, faces, slope, rows):
    for side, total in enumerate(convolve(pairs[0], weights[0])):
        mask = occ[x + side].reshape(256, 128).astype(F32)
        value = total * mask
        gate = jax.nn.sigmoid(value)
        hidden = value * gate
        slope[side] = gate * (1.0 + value * (1.0 - gate)) * mask
        keep_field(0, out_x + side, hidden, fields, turned, faces, rows)
    for side, total in enumerate(convolve(pairs[1], weights[1])):
        keep_field(1, out_x + side, total * slope[side], fields, turned, faces, rows)


def keep_field(arr, x, value, fields, turned, faces, rows):
    fields[arr, x] = value.astype(BF).reshape(8, 32, 128)
    columns = x * 256 if isinstance(x, int) else pl.multiple_of(x * 256, 256)
    turned[arr, :, pl.ds(columns, 256)] = value.T.astype(BF)
    z_faces(arr, x, value, rows, *faces)


def inner_kernel(main, y0, y1, e0, e1, z0, z1, occ, p1, t2, cat, fields, turned, q0, q1, rims, slope, rows):
    place = Places()
    gather_inner(place, cat, rims, (0, 1), 8, 0, main, y0, y1, e0, e1, 0, z0, z1)
    shift_slabs(place, cat, rims, 16, lambda i: i)

    def step(i, _):
        x = 2 + 2 * i
        pairs = [[cat.at[arr * 8 + x - 1 + k] for k in range(4)] for arr in range(2)]
        first_step(x, 2 * i, pairs, (p1, t2), occ, fields, turned, (q0, q1), slope, rows)
        return 0

    lax.fori_loop(0, 2, step, 0)


def outer_kernel(x0, x1, cat, part, part_turned, f0, f1, occ, p1, t2, ends, fields, turned, q0, q1, rims, slope, rows):
    place = Places()
    gather_outer(place, ends, rims, (0, 1), lambda at, end: at * 2 + spot_end(place, end), x0, x1)
    shift_slabs(place, ends, rims, 4, lambda i: i)
    fields[:, 2:6] = part[...]
    turned[:, :, 512:1536] = part_turned[...]
    for q, f in ((q0, f0), (q1, f1)):
        q[:, 2:6] = f[...]
    low = [[ends.at[arr * 2]] + [cat.at[arr * 8 + k] for k in range(3)] for arr in range(2)]
    high = [[cat.at[arr * 8 + 5 + k] for k in range(3)] + [ends.at[arr * 2 + 1]] for arr in range(2)]
    for x, pairs in ((0, low), (6, high)):
        first_step(x, x, pairs, (p1, t2), occ, fields, turned, (q0, q1), slope, rows)


def spot_end(place, slot):
    return place.odd[X] if slot else 1 - place.odd[X]


def grads_kernel(arr, cat, ends, turned, wide, thin):
    left = turned[1 - arr]

    def slab(a, x, b):
        at = x + a
        ref = ends.at[arr * 2 + at // 9] if at in (0, 9) else cat.at[arr * 8 + at - 1]
        return ref[b : b + 8].reshape(256, 384)

    taps = [(a, b) for a in range(3) for b in range(3)]
    for start in range(0, 9, 2):
        group = taps[start : start + 2]
        right = [jnp.concatenate([slab(a, x, b) for x in range(8)], axis=0) for a, b in group]
        right = jnp.concatenate(right, axis=1) if len(right) > 1 else right[0]
        value = jnp.dot(left, right, preferred_element_type=F32)
        columns = slice(start * 384, start * 384 + 384 * len(group))
        if arr:
            pieces = [value[h * 64 + y * 16 : h * 64 + y * 16 + 16] for y in range(4) for h in range(2)]
            value = jnp.concatenate(pieces, axis=0)
        value = value.reshape(4, 32, -1)
        wide[:, :, columns] = value
        thin[:, :, columns] = value.astype(BF)


def heavy_call(kernel, out_shape, operands, scratch, limit, flops):
    total = sum(v.size * v.dtype.itemsize for v in operands)
    single = not isinstance(out_shape, tuple)
    return pl.pallas_call(
        kernel,
        out_shape=out_shape,
        in_specs=[VMEM] * len(operands),
        out_specs=VMEM if single else (VMEM,) * len(out_shape),
        scratch_shapes=scratch,
        compiler_params=pltpu.CompilerParams(vmem_limit_bytes=limit * MIB),
        cost_estimate=pl.CostEstimate(flops=flops, bytes_accessed=total, transcendentals=0),
    )(*operands)


def first_pass(main, halos, occ, p1, t2):
    x0, x1, y0, y1, e0, e1, z0, z1 = halos

    def outs(count):
        face = shape_of((2, count, 8, 128), BF)
        return (shape_of((2, count, 8, 32, 128), BF), shape_of((2, 128, count * 256), BF), face, face)

    def scratch(slabs):
        return [
            pltpu.VMEM((2, slabs, 16, 128), F32),
            pltpu.VMEM((2, 256, 128), F32),
            pltpu.VMEM((256, 128), F32),
        ]

    cat, part, part_turned, f0, f1 = heavy_call(
        inner_kernel,
        (shape_of((16, 10, 32, 384), BF),) + outs(4),
        (main, y0, y1, e0, e1, z0, z1, occ, p1, t2),
        scratch(16), 6, 2_000_000_000,
    )
    ends, fields, turned, q0, q1 = heavy_call(
        outer_kernel,
        (shape_of((4, 10, 32, 384), BF),) + outs(8),
        (x0, x1, cat, part, part_turned, f0, f1, occ, p1, t2),
        scratch(4), 4, 2_000_000_000,
    )
    grad = (shape_of((4, 32, 27 * 128), F32), shape_of((4, 32, 27 * 128), BF))
    second, first = (
        heavy_call(functools.partial(grads_kernel, arr), grad, (cat, ends, turned), [], 4, 2_000_000_000)
        for arr in (1, 0)
    )
    return fields, (q0, q1), first, second


def second_kernel(arr, main, x0, x1, y0, y1, z0, z1, occ, weight, out, cat, rims):
    place = Places()
    gather_inner(place, cat, rims, (arr,), 10, 1, main, y0, y1, y0, y1, FACE, z0, z1)
    gather_outer(place, cat, rims, (arr,), lambda at, end: place.spot(X, end), x0, x1)
    shift_slabs(place, cat, rims, 10, lambda i: i)

    def step(i, _):
        slabs = [cat.at[2 * i + k] for k in range(4)]
        for side, total in enumerate(convolve(slabs, weight)):
            mask = occ[2 * i + side].reshape(256, 128).astype(F32)
            out[2 * i + side] = (total * mask).astype(BF).reshape(8, 32, 128)
        return 0

    lax.fori_loop(0, 4, step, 0)


def second_pass(arr, main, halos, occ, weight):
    return heavy_call(
        functools.partial(second_kernel, arr),
        shape_of((8, 8, 32, 128), BF),
        (main, *halos, occ, weight),
        [pltpu.VMEM((10, 10, 32, 384), BF), pltpu.VMEM((2, 10, 16, 128), F32)],
        8, 2_000_000_000,
    )


def swap_faces(values, axis, slot):
    pairs = []
    for number in range(128):
        at = [number // 16, number // 4 % 4, number % 4]
        count, i = (8, 4, 4)[axis], at[axis]
        if slot == 0:
            at[axis] = i ^ 1
        elif axis == Z or 0 < i < count - 1:
            at[axis] = (i - 1 + 2 * (i % 2)) % count
        else:
            at[Z] ^= 1
        pairs.append((number, at[0] * 16 + at[1] * 4 + at[2]))
    return lax.ppermute(values, AXES, pairs)


def small_call(kernel, out_shape, operands, scratch=(), limit=2, inputs=None):
    single = not isinstance(out_shape, tuple)
    total = sum(v.size * v.dtype.itemsize for v in operands)
    return pl.pallas_call(
        kernel,
        out_shape=out_shape,
        in_specs=inputs or [VMEM] * len(operands),
        out_specs=VMEM if single else (VMEM,) * len(out_shape),
        scratch_shapes=scratch,
        compiler_params=pltpu.CompilerParams(vmem_limit_bytes=limit * MIB),
        cost_estimate=pl.CostEstimate(flops=0, bytes_accessed=total, transcendentals=0),
    )(*operands)


def z_faces(arr, x, values, rows, m0, m1):
    odd = place_on(Z)[1]
    rows[...] = values
    m0[arr, x] = rows[pl.ds(31 - 31 * odd, 8, stride=32), :].astype(BF)
    m1[arr, x] = rows[pl.ds(31 * odd, 8, stride=32), :].astype(BF)


def mask_kernel(bricks_far, features, cotangent, mask_far, main, occ, m0, m1, f0, f1, held, rows, mask, bricks, arrived, ready):
    flags_in = pltpu.make_async_copy(mask_far, mask, ready.at[0])
    bricks_in = pltpu.make_async_copy(bricks_far, bricks, ready.at[1])
    flags_in.start()
    bricks_in.start()
    copies = [
        [
            pltpu.make_async_copy(
                source.at[pl.ds(half * 4, 4)], held.at[arr, pl.ds(half * 4, 4)], arrived.at[arr, half]
            )
            for arr, source in ((0, features), (1, cotangent))
        ]
        for half in range(2)
    ]
    for pair in copies:
        for copy in pair:
            copy.start()
    flags_in.wait()
    bricks_in.wait()
    lane = lax.broadcasted_iota(jnp.int32, (8, 32), 1)
    active = jnp.zeros((8, 32), jnp.int32)
    for k in range(4):
        active = jnp.where(lane // BRICK == k, bricks[0, 0, k], active)
    diagonal = lax.broadcasted_iota(jnp.int32, (32, 32), 0) == lax.broadcasted_iota(jnp.int32, (32, 32), 1)
    ones = jnp.ones((32, 128), BF)
    for x in range(8):
        flags = (mask[x] * active).astype(F32)
        spread = [
            jnp.where(diagonal, jnp.broadcast_to(flags[y : y + 1], (32, 32)), 0.0) for y in range(8)
        ]
        wide = jnp.dot(jnp.concatenate(spread).astype(BF), ones, preferred_element_type=F32)
        occ[x] = wide.astype(BF).reshape(8, 32, 128)
    odd = place_on(Y)[1]
    for x in range(8):
        if x % 4 == 0:
            for copy in copies[x // 4]:
                copy.wait()
        wide = occ[x].reshape(256, 128).astype(F32)
        for arr in range(2):
            masked = held[arr, x].reshape(256, 128).astype(F32) * wide
            main[arr, x] = masked.astype(BF).reshape(8, 32, 128)
            z_faces(arr, x, masked, rows, m0, m1)
            row = arr * 256 + x * 32
            f0[row : row + 32, :] = main[arr, x, 7 - 7 * odd]
            f1[row : row + 32, :] = main[arr, x, 7 * odd]


def mask_inputs(features, cotangent, voxel_mask, brick_active):
    z_message, y_message = shape_of((2, 8, 8, 128), BF), shape_of((FACE, 128), BF)
    far = pl.BlockSpec(memory_space=pltpu.HBM)
    return small_call(
        mask_kernel,
        (shape_of((2, 8, 8, 32, 128), BF), shape_of((8, 8, 32, 128), BF), z_message, z_message, y_message, y_message),
        [
            pltpu.with_memory_space_constraint(v, pltpu.HBM)
            for v in (brick_active, features, cotangent, voxel_mask)
        ],
        scratch=[
            pltpu.VMEM((2, 8, 8, 32, 128), BF),
            pltpu.VMEM((256, 128), F32),
            pltpu.VMEM((8, 8, 32), jnp.int32),
            pltpu.SMEM((1, 1, 4), jnp.int32),
            pltpu.SemaphoreType.DMA((2, 2)),
            pltpu.SemaphoreType.DMA((2,)),
        ],
        limit=4,
        inputs=[far] * 4,
    )


def y_kernel(main, z0, z1, m0, m1, own):
    odd = place_on(Y)[1]
    for slot, rims in ((0, z0), (1, z1)):
        own[slot] = rims[...].astype(F32).reshape(128, 128)
    for out, y in ((m0, 7 - 7 * odd), (m1, 7 * odd)):
        for arr in range(2):
            out[arr * 256 : arr * 256 + 256, :] = main[arr, :, y].reshape(256, 128)
            for slot in range(2):
                row = FACE + slot * 16 + arr * 8
                out[row : row + 8, :] = own[slot, pl.ds(arr * 64 + y, 8, stride=8), :].astype(BF)


def edge_kernel(z0, z1, m0, m1, own):
    odd = place_on(Y)[1]
    for slot, rims in ((0, z0), (1, z1)):
        own[slot] = rims[...].astype(F32).reshape(128, 128)
    for out, y in ((m0, 7 - 7 * odd), (m1, 7 * odd)):
        for arr in range(2):
            for slot in range(2):
                row = slot * 16 + arr * 8
                out[row : row + 8, :] = own[slot, pl.ds(arr * 64 + y, 8, stride=8), :].astype(BF)


def x_kernel(edge, main, y0, y1, e0, e1, z0, z1, m0, m1, ends, piece):
    odd = place_on(X)[1]
    piece[...] = jnp.zeros_like(piece)
    for side, face in ((0, e0), (1, e1)):
        ends[side] = face[edge : edge + 32, :].astype(F32)
    for out, x in ((m0, 7 - 7 * odd), (m1, 7 * odd)):
        for arr in range(2):
            out[arr * 256 : arr * 256 + 256, :] = main[arr, x].reshape(256, 128)
            for side, face in ((0, y0), (1, y1)):
                row = FACE + side * 64 + arr * 32
                from_row = pl.multiple_of(arr * 256 + x * 32, 32)
                out[row : row + 32, :] = face[pl.ds(from_row, 32), :]
            for slot, rims in ((0, z0), (1, z1)):
                at = slot * 16 + arr * 8
                piece[0:1, :] = ends[0, pl.ds(at + x, 1), :]
                piece[1:9, :] = rims[arr, x].astype(F32)
                piece[9:10, :] = ends[1, pl.ds(at + x, 1), :]
                row = FACE + 128 + slot * 32 + arr * 16
                out[row : row + 16, :] = piece[...].astype(BF)


def exchange_x(main, y0, y1, e0, e1, edge, z0, z1):
    messages = small_call(
        functools.partial(x_kernel, edge),
        (shape_of((704, 128), BF),) * 2,
        (main, y0, y1, e0, e1, z0, z1),
        scratch=[pltpu.VMEM((2, 32, 128), F32), pltpu.VMEM((16, 128), F32)],
    )
    x0 = swap_faces(messages[0], X, 0)
    x1 = swap_faces(messages[1], X, 1)
    return x0, x1


def exchange_first(main, messages, faces):
    z0 = swap_faces(messages[0], Z, 0)
    z1 = swap_faces(messages[1], Z, 1)
    y0 = swap_faces(faces[0], Y, 0)
    y1 = swap_faces(faces[1], Y, 1)
    edges = small_call(edge_kernel, (shape_of((32, 128), BF),) * 2, (z0, z1), scratch=[pltpu.VMEM((2, 128, 128), F32)])
    e0 = swap_faces(edges[0], Y, 0)
    e1 = swap_faces(edges[1], Y, 1)
    x0, x1 = exchange_x(main, y0, y1, e0, e1, 0, z0, z1)
    return x0, x1, y0, y1, e0, e1, z0, z1


def exchange_second(main, messages):
    z0 = swap_faces(messages[0], Z, 0)
    z1 = swap_faces(messages[1], Z, 1)
    messages = small_call(
        y_kernel, (shape_of((544, 128), BF),) * 2, (main, z0, z1), scratch=[pltpu.VMEM((2, 128, 128), F32)]
    )
    y0 = swap_faces(messages[0], Y, 0)
    y1 = swap_faces(messages[1], Y, 1)
    x0, x1 = exchange_x(main, y0, y1, y0, y1, FACE, z0, z1)
    return x0, x1, y0, y1, z0, z1


def device_places():
    places = []
    for number in range(128):
        gx, gy, gz = number // 16, number // 4 % 4, number % 4
        places.append(((gx // 4) * 2 + gz // 2, gx % 4, gy, gz % 2))
    return places


def permute_chips(values, move):
    places = device_places()
    index = {place: number for number, place in enumerate(places)}
    pairs = [(n, index[move(*place)]) for n, place in enumerate(places)]
    return lax.ppermute(values, AXES, pairs)


def swap_cores(values):
    return permute_chips(values, lambda x, y, z, c: (x, y, z, 1 - c))


PARTNERS = (2, 1, 3)


def along_rows(flip):
    return lambda x, y, z, c: (x, y ^ (flip * c), z ^ (flip * (1 - c)), c)


def along_lanes(flip):
    return lambda x, y, z, c: (x, y ^ (flip * (1 - c)), z ^ (flip * c), c)


def along_x(flip):
    return lambda x, y, z, c: (x ^ flip, y, z, c)


def split_kernel(first, got_first, second, got_second, own, m1, m2, m3):
    _, y, z, core = chip_place()
    for which, block, keep, got in ((0, z, first, got_first), (1, y, second, got_second)):

        @pl.when(core == which)
        def _():
            for flip, out in zip((0,) + PARTNERS, (own, m1, m2, m3)):
                at = block ^ flip
                out[...] = (keep[at] + got[at].astype(F32)).astype(out.dtype)


def total_of(own, parts):
    r1, r2, r3 = (part[...].astype(F32) for part in parts)
    return own[...] + (r1 + r2) + r3


def halves_kernel(own, r1, r2, r3, kept, m1, m2, m3, whole):
    x, _, _, core = chip_place()
    whole[...] = total_of(own, (r1, r2, r3))
    for flip, out in zip((0,) + PARTNERS, (kept, m1, m2, m3)):
        chip = x ^ flip
        half = jnp.where(core == 0, chip & 1, chip >> 1)
        out[...] = whole[pl.ds(pl.multiple_of(half * 16, 16), 16), :].astype(out.dtype)


def sum_kernel(own, r1, r2, r3, total, message):
    value = total_of(own, (r1, r2, r3))
    total[...] = value
    message[...] = value.astype(BF)


def piece_kernel(factor, own, r1, r2, r3, piece):
    x, y, z, core = chip_place()
    block = jnp.where(core == 0, (x >> 1) * 4 + y, z * 2 + (x & 1))
    value = total_of(own, (r1, r2, r3)) * factor
    shift = (128 - block * 16) & 127
    for tap in range(27):
        at = jnp.where(core == 0, tap, 26 - tap)
        piece[at] = pltpu.roll(value[:, tap * 128 : tap * 128 + 128], shift, 1)
    for tap in range(27, 32):
        piece[tap] = jnp.zeros((16, 128), F32)


def outputs_kernel(mine, other, first, second, both):
    core = chip_place()[3]
    both[core] = mine[...].reshape(512, 128)
    both[1 - core] = other[...].reshape(512, 128)
    for j in range(8):
        turned = both[0, pl.ds(core * 8 + j, 32, stride=16), :].T
        first[pl.ds(j, 16, stride=8), :] = turned[0:16, 0:27]
    for i in range(16):
        turned = both[1, pl.ds(i, 32, stride=16), :].T
        second[i * 8 : i * 8 + 8, :] = jnp.where(core == 0, turned[0:8, 0:27], turned[8:16, 0:27])


def reduce_grads(first, second, factor):
    lanes = 27 * 128
    wide, thin = shape_of((32, lanes), BF), shape_of((16, lanes), BF)
    got_second = swap_cores(second[1])
    got_first = swap_cores(first[1])
    own, *messages = small_call(
        split_kernel, (shape_of((32, lanes), F32), wide, wide, wide), (first[0], got_first, second[0], got_second)
    )
    parts = [permute_chips(m, along_rows(PARTNERS[i])) for i, m in enumerate(messages)]
    own, *messages = small_call(
        halves_kernel,
        (shape_of((16, lanes), F32), thin, thin, thin),
        (own, *parts),
        scratch=[pltpu.VMEM((32, lanes), F32)],
    )
    parts = [permute_chips(m, along_x(PARTNERS[i])) for i, m in enumerate(messages)]
    own, message = small_call(sum_kernel, (shape_of((16, lanes), F32), thin), (own, *parts))
    parts = [permute_chips(message, along_lanes(PARTNERS[i])) for i in range(3)]
    piece = small_call(functools.partial(piece_kernel, factor), shape_of((32, 16, 128), F32), (own, *parts))
    other = swap_cores(piece)
    first, second = small_call(
        outputs_kernel, (shape_of((128, 27), F32),) * 2, (piece, other), scratch=[pltpu.VMEM((2, 512, 128), F32)]
    )
    return tuple(jnp.transpose(g.reshape(16, 8, 27), (2, 0, 1)) for g in (first, second))


def on_device(features, cotangent, voxel_mask, brick_active, first_weight, second_weight):
    factor = 1.0 / math.sqrt(voxel_mask.size * 128)
    main, occ, m0, m1, f0, f1 = mask_inputs(features, cotangent, voxel_mask, brick_active)
    p1, t2 = prepare_weights(first_weight, second_weight)
    p2, t1 = prepare_weights(second_weight, first_weight)
    fields, next_faces, first, second = first_pass(main, exchange_first(main, (m0, m1), (f0, f1)), occ, p1, t2)
    halos = exchange_second(fields, next_faces)
    grad_first, grad_second = reduce_grads(first, second, factor)
    output_field = second_pass(0, fields, halos, occ, p2)
    grad_features = second_pass(1, fields, halos, occ, t1)
    return (output_field, grad_features, grad_first, grad_second)


def solution(mesh):
    return jax.shard_map(
        on_device,
        mesh=mesh,
        in_specs=(
            P("gx", "gy", "gz", None),
            P("gx", "gy", "gz", None),
            P("gx", "gy", "gz"),
            P("gx", "gy", "gz"),
            P(),
            P(),
        ),
        out_specs=(
            P("gx", "gy", "gz", None),
            P("gx", "gy", "gz", None),
            P(None, "gx", ("gy", "gz")),
            P(None, "gx", ("gy", "gz")),
        ),
        check_vma=False,
    )
```
